32 devices in a mesh: grp: 2 (over y), smp: 4 (over z), blk: 2 (over x), pen: 2 (over core).
Axes of the slice: x: 2, y: 2, z: 4, core: 2. Of those that a mesh axis runs over, the one named last changes fastest.
Arguments:
- allele_matrix: bfloat16 [2048, 4096], P('smp', ('grp', 'blk')), parts along dimension 1, may hold values from -6 to 6
- orthonormal_frames: bfloat16 [8, 512, 512], P(('grp', 'blk')), parts along dimension 0, may hold values from -0.25 to 0.25
- segment_variances: float32 [8, 512], P(('grp', 'blk')), parts along dimension 0, may hold values from 20.48 to 2048
- lambda_grid: float32 [4], replicated, may hold values from 20.48 to 2048
- trait_levels: bfloat16 [2048, 256], P('smp', ('grp', 'pen')), parts along dimension 1, may hold values from -6 to 6
- partition_labels: int32 [2048], P('smp'), may hold values from 0 to 3
- preceding_fits: bfloat16 [4, 2048, 1536], P(('grp', 'pen'), 'smp', 'blk'), parts along dimension 0, may hold values from -6 to 6
Outputs:
- level0_predictions: bfloat16 [2048, 8, 4, 128], P('smp', ('grp', 'blk'), None, 'pen'), parts along dimension 1
- gram_old: float32 [4, 1536, 1536], P(('grp', 'pen'), 'blk', 'smp'), parts along dimension 0
- gram_cross: float32 [4, 16, 1536], P(('grp', 'pen'), 'blk', 'smp'), parts along dimension 0
- gram_new: float32 [4, 16, 16], P(('grp', 'pen'), 'blk'), parts along dimension 0
- fit_old: float32 [4, 1536], P(('grp', 'pen'), 'smp'), parts along dimension 0
- fit_new: float32 [4, 16], P(('grp', 'pen'), 'blk'), parts along dimension 0
The draws below stay inside these ranges and needn't reach their ends.
There are 2 independent parts, one for each index of `grp`. The reference program is written for one: setup_inputs(seed, part) draws one part's arguments, and reference() takes and returns one part's arrays. A program takes and returns all parts, laid end to end along the dimension named above; an argument that names none is the same for every part. Nothing has to cross between parts.
All inputs are finite; a program needn't handle non-finite values.
Results may differ from the reference program's by a relative error of at most 0.018.
Values may be sent and summed in bfloat16 or wider, within the bound.
A program may use at most 64 MiB of HBM per device.

```python
import math
import jax
import jax.numpy as jnp
from jax import lax

VARIANT_COUNT = 512
PROTEIN_COUNT = 128
LAMBDA_GRID_SIZE = 4
FOLDS = 4
EARLIER = 1536
SAMPLE_TOTAL = 2048
BLOCK_TOTAL = 4


def plant(result, stream_key, smallest, largest):
    longest = result.shape.index(max(result.shape))
    spots = []
    for shift in (0, 1):
        where = [jax.random.randint(jax.random.fold_in(stream_key, axis), (), 0, length) for axis, length in enumerate(result.shape)]
        where[longest] = (where[longest] + shift) % result.shape[longest]
        spots.append(tuple(where))
    return result.at[spots[0]].set(smallest).at[spots[1]].set(largest)


def block_scale(key, shape, shards, smallest, top_value):
    def one(position, shards_of):
        draws = jax.random.uniform(jax.random.fold_in(jax.random.fold_in(key, 6), position), (shards_of,), jnp.float32, smallest / len(shards), top_value / len(shards))
        return jnp.repeat(jnp.exp(draws), shape[position] // shards_of).reshape((-1,) + (1,) * (len(shape) - position - 1))

    loudness = one(*shards[0])
    for cut in shards[1:]:
        loudness = loudness * one(*cut)
    return loudness


def gaussian(key, dims, deviation, reach, shards=(), held_as=jnp.bfloat16):
    level = block_scale(key, dims, shards, -0.22, 0.18) if shards else 1.0
    array = jax.random.normal(key, dims, jnp.float32) * deviation * level
    return jnp.minimum(jnp.maximum(array, -reach), reach).astype(held_as)


def setup_inputs(seed: int = 0, part: int = 0) -> dict:
    arg_keys = jax.random.split(jax.random.key(seed), 8)
    part_splits = jax.random.split(jax.random.fold_in(arg_keys[7], part), 8)
    allele_matrix = gaussian(part_splits[0], (SAMPLE_TOTAL, BLOCK_TOTAL * VARIANT_COUNT), 1.0, 6.0, ((0, 4), (1, 2)))
    orthonormal_frames = gaussian(part_splits[1], (BLOCK_TOTAL, VARIANT_COUNT, VARIANT_COUNT), VARIANT_COUNT ** -0.5, 0.25, ((0, 2),))
    segment_variances = jnp.clip(jnp.exp(math.log(2048.0) - 4.6051702 * jax.random.uniform(part_splits[2], (BLOCK_TOTAL, VARIANT_COUNT), jnp.float32) ** block_scale(part_splits[2], (BLOCK_TOTAL, VARIANT_COUNT), ((0, 2),), -0.2, 0.2)), 20.48, 2048.0)
    lambda_grid = jnp.clip(jnp.exp(jax.random.uniform(arg_keys[3], (LAMBDA_GRID_SIZE,), jnp.float32, math.log(20.48), math.log(2048.0))), 20.48, 2048.0)
    trait_levels = gaussian(part_splits[4], (SAMPLE_TOTAL, PROTEIN_COUNT), 1.0, 6.0, ((0, 4), (1, 2)))
    partition_labels = plant(jax.random.randint(arg_keys[5], (SAMPLE_TOTAL,), 0, FOLDS), jax.random.fold_in(arg_keys[5], 1), 0, FOLDS - 1).astype(jnp.int32)
    preceding_fits = gaussian(part_splits[6], (2, SAMPLE_TOTAL, EARLIER), 1.0, 6.0, ((0, 2), (1, 4), (2, 2)))
    return {"allele_matrix": allele_matrix, "orthonormal_frames": orthonormal_frames, "segment_variances": segment_variances, "lambda_grid": lambda_grid, "trait_levels": trait_levels, "partition_labels": partition_labels, "preceding_fits": preceding_fits}


def segment_fitted_trait(projected_traits, pairwise_inner, spectral_line, lambda_grid, partition_mask_real):
    remainder = jnp.sum(pairwise_inner, axis=1, keepdims=True) - pairwise_inner
    damping_ratio = 1.0 / (spectral_line[:, None] + lambda_grid[None, :])
    ridge_coefficients = (remainder[:, :, None, :] * damping_ratio[:, None, :, None]).astype(jnp.bfloat16)
    samples_number = projected_traits.shape[0]
    running_total = jnp.zeros((samples_number, LAMBDA_GRID_SIZE * PROTEIN_COUNT), jnp.float32)
    for holdout_index in range(FOLDS):
        lookup_table = ridge_coefficients[:, holdout_index].reshape(VARIANT_COUNT, LAMBDA_GRID_SIZE * PROTEIN_COUNT)
        running_total = running_total + partition_mask_real[:, holdout_index:holdout_index + 1] * jnp.dot(projected_traits, lookup_table, preferred_element_type=jnp.float32)
    return running_total.reshape(samples_number, LAMBDA_GRID_SIZE, PROTEIN_COUNT).astype(jnp.bfloat16)


def reference(allele_matrix, orthonormal_frames, segment_variances, lambda_grid, trait_levels, partition_labels, preceding_fits):
    member = partition_labels[:, None] == jnp.arange(FOLDS, dtype=jnp.int32)[None, :]
    partition_mask_real = member.astype(jnp.float32)
    masked = (member.astype(jnp.bfloat16)[:, :, None] * trait_levels[:, None, :]).reshape(SAMPLE_TOTAL, FOLDS * PROTEIN_COUNT)

    def one_block(entry_offset):
        start = (entry_offset * VARIANT_COUNT).astype(jnp.int32)
        genotype_cols = lax.dynamic_slice_in_dim(allele_matrix, start, VARIANT_COUNT, 1)
        projected_traits = jnp.dot(genotype_cols, orthonormal_frames[entry_offset], preferred_element_type=jnp.float32).astype(jnp.bfloat16)
        pairwise_inner = jnp.dot(projected_traits.T, masked, preferred_element_type=jnp.float32).reshape(VARIANT_COUNT, FOLDS, PROTEIN_COUNT)
        return segment_fitted_trait(projected_traits, pairwise_inner, segment_variances[entry_offset], lambda_grid, partition_mask_real)

    stacked = lax.map(one_block, jnp.arange(BLOCK_TOTAL, dtype=jnp.int32))
    level0_predictions = jnp.transpose(stacked, (1, 0, 2, 3))
    half_width = PROTEIN_COUNT // 2
    olds, crosses, news, fit_olds, fit_news = [], [], [], [], []
    for choice_index in range(2):
        column_slot = choice_index * half_width
        added_columns = level0_predictions[:, :, :, column_slot].reshape(SAMPLE_TOTAL, BLOCK_TOTAL * LAMBDA_GRID_SIZE)
        target = trait_levels[:, column_slot:column_slot + 1]
        old_cols = preceding_fits[choice_index]
        olds.append(jnp.dot(old_cols.T, old_cols, preferred_element_type=jnp.float32) / SAMPLE_TOTAL)
        crosses.append(jnp.dot(added_columns.T, old_cols, preferred_element_type=jnp.float32) / SAMPLE_TOTAL)
        news.append(jnp.dot(added_columns.T, added_columns, preferred_element_type=jnp.float32) / SAMPLE_TOTAL)
        fit_olds.append(jnp.dot(old_cols.T, target, preferred_element_type=jnp.float32)[:, 0] / SAMPLE_TOTAL)
        fit_news.append(jnp.dot(added_columns.T, target, preferred_element_type=jnp.float32)[:, 0] / SAMPLE_TOTAL)
    return (level0_predictions, jnp.stack(olds), jnp.stack(crosses), jnp.stack(news), jnp.stack(fit_olds), jnp.stack(fit_news))
```

```python
import functools
import math

import jax
import jax.numpy as jnp
from jax import lax
from jax.experimental import pallas as pl
from jax.experimental.pallas import tpu as pltpu
from jax.sharding import PartitionSpec as P

FOLDS = 4
F32 = jnp.float32
BF16 = jnp.bfloat16
MESH = pl.DeviceIdType.MESH


def row_piece(total):
    return next(size for size in (256, 128) if total % size == 0)


def kernel(
    n, nb, groups,
    allele, frames, variances, lam, trait, labels, old,
    preds_out, gram_out, cross_out, new_out, fit_old_out, fit_new_out,
    oldq, old_t, rot, part, c_left, c_right, c_send,
    g_left, g_right, g_send, g_part, et_all, lhs, m_send, m_recv, m_sum,
    x_send, x_recv, cs_send, cs_recv, gs_send, gl_recv, gr_recv,
    e_send, e_recv, ms_send, ms_recv,
):
    z = lax.axis_index("smp")
    x = lax.axis_index("blk")
    rows, old_width = old.shape
    blocks, width = frames.shape[0], frames.shape[1]
    prot = trait.shape[1]
    lams = groups
    per = n // nb
    qw = old_width // per
    cp = row_piece(blocks * width)
    c_pieces = blocks * width // cp
    gp = row_piece(old_width)
    g_pieces = old_width // gp
    new_width = blocks * lams
    erows = et_all.shape[1]
    sample_total = float(rows * n)
    order = []
    for i in range(n // 2):
        order += [n - 1 - i, i]

    barrier = pltpu.get_barrier_semaphore()
    for d in range(1, n):
        pl.semaphore_signal(barrier, inc=1, device_id={"smp": lax.rem(z + d, n)}, device_id_type=MESH)
    for d in range(1, nb):
        pl.semaphore_signal(barrier, inc=1, device_id={"blk": lax.rem(x + d, nb)}, device_id_type=MESH)
    pl.semaphore_wait(barrier, n - 1 + nb - 1)

    def x_copy(q, d):
        cols = pl.ds(pl.multiple_of((q - x * per) * qw, qw), qw)
        return pltpu.make_async_remote_copy(
            src_ref=old.at[:, cols], dst_ref=oldq.at[q], send_sem=x_send.at[q, d], recv_sem=x_recv.at[q],
            device_id={"blk": lax.rem(x + d, nb)}, device_id_type=MESH)

    def x_wait(q):
        pltpu.make_async_remote_copy(
            src_ref=oldq.at[q], dst_ref=oldq.at[q], send_sem=x_send.at[q, 0], recv_sem=x_recv.at[q],
            device_id={"blk": lax.rem(x + 1, nb)}, device_id_type=MESH).wait_recv()

    for q in order:
        @pl.when(x == q // per)
        def _():
            for d in range(1, nb):
                x_copy(q, d).start()

    label = labels[...]
    y = trait[...]
    y_wide = jnp.concatenate([y] * FOLDS, axis=1)
    fold_of = lax.broadcasted_iota(jnp.int32, (rows, FOLDS * prot), 1) // prot
    masked = jnp.where(label == fold_of, y_wide.astype(F32), 0.0).astype(BF16)

    def c_copy(p, right):
        piece = pl.ds(p * cp, cp)
        return pltpu.make_async_remote_copy(
            src_ref=c_send.at[0 if right else 1, piece, :],
            dst_ref=(c_left if right else c_right).at[piece, :],
            send_sem=cs_send.at[0 if right else 1, p], recv_sem=cs_recv.at[0 if right else 1, p],
            device_id={"smp": jnp.minimum(z + 1, n - 1) if right else jnp.maximum(z - 1, 0)}, device_id_type=MESH)

    for b in range(blocks):
        r = jnp.dot(allele[:, b * width:(b + 1) * width], frames[b], preferred_element_type=F32).astype(BF16)
        rot[b] = r
        part[b * width:(b + 1) * width, :] = lax.dot_general(
            r, masked, (((0,), (0,)), ((), ())), preferred_element_type=F32)
        for p in range(b * width // cp, (b + 1) * width // cp):
            value = part[p * cp:(p + 1) * cp, :].astype(BF16)

            @pl.when(z == 0)
            def _():
                c_send[0, p * cp:(p + 1) * cp, :] = value
                c_copy(p, True).start()

            @pl.when(z == n - 1)
            def _():
                c_send[1, p * cp:(p + 1) * cp, :] = value
                c_copy(p, False).start()

    for h in range(per):
        oldq[x * per + h] = old[:, h * qw:(h + 1) * qw]
    old_t[...] = old[...].T
    for q in order:
        @pl.when(x != q // per)
        def _():
            x_wait(q)

    def g_copy(q, h, right):
        piece = pl.ds(pl.multiple_of(h * gp, gp), gp)
        return pltpu.make_async_remote_copy(
            src_ref=g_send.at[q, piece, :],
            dst_ref=(g_left if right else g_right).at[q, piece, :],
            send_sem=gs_send.at[q, h], recv_sem=(gl_recv if right else gr_recv).at[q, h],
            device_id={"smp": jnp.minimum(z + 1, n - 1) if right else jnp.maximum(z - 1, 0)}, device_id_type=MESH)

    def g_piece(q, h):
        piece = pl.ds(pl.multiple_of(h * gp, gp), gp)
        g_part[...] = jnp.dot(old_t[piece, :], oldq[q], preferred_element_type=F32)

        @pl.when(z < q)
        def _():
            @pl.when(z > 0)
            def _():
                g_copy(q, h, True).wait_recv()
                g_part[...] += g_left[q, piece, :].astype(F32)
            g_send[q, piece, :] = g_part[...].astype(BF16)
            g_copy(q, h, True).start()

        @pl.when(z > q)
        def _():
            @pl.when(z < n - 1)
            def _():
                g_copy(q, h, False).wait_recv()
                g_part[...] += g_right[q, piece, :].astype(F32)
            g_send[q, piece, :] = g_part[...].astype(BF16)
            g_copy(q, h, False).start()

        @pl.when(z == q)
        def _():
            @pl.when(z > 0)
            def _():
                g_copy(q, h, True).wait_recv()
                g_part[...] += g_left[q, piece, :].astype(F32)

            @pl.when(z < n - 1)
            def _():
                g_copy(q, h, False).wait_recv()
                g_part[...] += g_right[q, piece, :].astype(F32)
            gram_out[piece, :] = g_part[...] / sample_total

    def g_group(q):
        def body(h, carry):
            g_piece(q, h)
            return carry
        lax.fori_loop(0, g_pieces, body, 0)

    in_left = z < n // 2
    is_end = jnp.logical_or(z == 0, z == n - 1)

    @pl.when(is_end)
    def _():
        g_group(jnp.where(in_left, n - 1, 0))

    def from_side(p, right):
        piece = slice(p * cp, (p + 1) * cp)
        has = z > 0 if right else z < n - 1
        forward = z < n - 1 if right else z > 0

        @pl.when(has)
        def _():
            c_copy(p, right).wait_recv()

            @pl.when(forward)
            def _():
                got = (c_left if right else c_right)[piece, :]
                c_send[0 if right else 1, piece, :] = (part[piece, :] + got.astype(F32)).astype(BF16)
                c_copy(p, right).start()

    for first in (True, False):
        for p in range(c_pieces):
            @pl.when(in_left)
            def _():
                from_side(p, first)

            @pl.when(jnp.logical_not(in_left))
            def _():
                from_side(p, not first)

    @pl.when(z > 0)
    def _():
        part[...] += c_left[...].astype(F32)

    @pl.when(z < n - 1)
    def _():
        part[...] += c_right[...].astype(F32)

    lam_lane = lax.broadcasted_iota(jnp.int32, (1, lams * prot), 1) // prot
    lam_wide = jnp.zeros((1, lams * prot), F32)
    for r in range(lams):
        lam_wide = jnp.where(lam_lane == r, lam[r], lam_wide)
    sel_rows = lax.broadcasted_iota(jnp.int32, (erows, lams * prot), 0)
    sel_cols = lax.broadcasted_iota(jnp.int32, (erows, lams * prot), 1)
    e0 = jnp.zeros((erows, rows), F32)
    for b in range(blocks):
        damp = 1.0 / (variances[:, b:b + 1] + lam_wide)
        c = part[b * width:(b + 1) * width, :]
        folds = [c[:, k * prot:(k + 1) * prot] for k in range(FOLDS)]
        total = folds[0]
        for k in range(1, FOLDS):
            total = total + folds[k]
        acc = jnp.zeros((rows, lams * prot), F32)
        for k in range(FOLDS):
            rest = jnp.concatenate([total - folds[k]] * lams, axis=1)
            coeff = (rest * damp).astype(BF16)
            acc = jnp.where(label == k, jnp.dot(rot[b], coeff, preferred_element_type=F32), acc)
        pred = acc.astype(BF16)
        preds_out[:, b * lams * prot:(b + 1) * lams * prot] = pred
        wanted = x * new_width + b * lams + sel_cols // prot
        sel = jnp.where(jnp.logical_and(sel_rows == wanted, sel_cols % prot == 0), 1.0, 0.0).astype(BF16)
        e0 = e0 + lax.dot_general(sel, pred, (((1,), (1,)), ((), ())), preferred_element_type=F32)
    et_all[x] = e0.astype(BF16)

    def e_copy(d):
        return pltpu.make_async_remote_copy(
            src_ref=et_all.at[x], dst_ref=et_all.at[x], send_sem=e_send.at[d], recv_sem=e_recv.at[d],
            device_id={"blk": lax.rem(x + d, nb)}, device_id_type=MESH)

    def e_wait(d):
        slot = lax.rem(x + nb - d, nb)
        pltpu.make_async_remote_copy(
            src_ref=et_all.at[slot], dst_ref=et_all.at[slot], send_sem=e_send.at[d], recv_sem=e_recv.at[d],
            device_id={"blk": slot}, device_id_type=MESH).wait_recv()

    for d in range(1, nb):
        e_copy(d).start()
    t_rows = lax.broadcasted_iota(jnp.int32, (erows, prot), 0)
    t_cols = lax.broadcasted_iota(jnp.int32, (erows, prot), 1)
    t_sel = jnp.where(jnp.logical_and(t_rows == nb * new_width, t_cols == 0), 1.0, 0.0).astype(BF16)
    target = lax.dot_general(t_sel, y, (((1,), (1,)), ((), ())), preferred_element_type=F32)
    lhs[...] = (e0 + target).astype(BF16)
    for q in range(n):
        m_send[q, :, :qw] = jnp.dot(lhs[...], oldq[q], preferred_element_type=F32)
    for d in range(1, nb):
        e_wait(d)
    right_side = target
    for b in range(nb):
        right_side = right_side + et_all[b].astype(F32)
    small = lax.dot_general(
        lhs[...], jnp.concatenate([right_side.astype(BF16), jnp.zeros((128 - erows, rows), BF16)], axis=0),
        (((1,), (1,)), ((), ())), preferred_element_type=F32)
    for q in range(n):
        m_send[q, :, qw:] = small

    def m_copy(d):
        return pltpu.make_async_remote_copy(
            src_ref=m_send.at[lax.rem(z + d, n)], dst_ref=m_recv.at[d], send_sem=ms_send.at[d], recv_sem=ms_recv.at[d],
            device_id={"smp": lax.rem(z + d, n)}, device_id_type=MESH)

    for d in range(1, n):
        m_copy(d).start()

    for i in range(n // 2):
        early = jnp.where(in_left, n - 1 - i, i)
        late = n - 1 - early
        if i == 0:
            @pl.when(jnp.logical_not(is_end))
            def _():
                g_group(early)
        else:
            @pl.when(early != z)
            def _():
                g_group(early)

        @pl.when(late != z)
        def _():
            g_group(late)
    g_group(z)

    total = m_send[z]
    for d in range(1, n):
        m_copy(d).wait_recv()
        total = total + m_recv[d]
    m_sum[...] = total / sample_total
    mine = pl.ds(pl.multiple_of(x * new_width, 8), new_width)
    cross_out[...] = m_sum[mine, :qw]
    tail = m_sum[mine, qw:]
    new_out[...] = tail[:, :nb * new_width]
    lane = lax.broadcasted_iota(jnp.int32, tail.shape, 1)
    fit_new_out[...] = jnp.sum(jnp.where(lane == nb * new_width, tail, 0.0), axis=1, keepdims=True)
    fit_old_out[...] = m_sum[nb * new_width:nb * new_width + 1, :qw]

    for q in range(n):
        @pl.when(x == q // per)
        def _():
            for d in range(1, nb):
                x_copy(q, d).wait_send()
    for p in range(c_pieces):
        @pl.when(z < n - 1)
        def _():
            c_copy(p, True).wait_send()

        @pl.when(z > 0)
        def _():
            c_copy(p, False).wait_send()
    for d in range(1, nb):
        e_copy(d).wait_send()
    for d in range(1, n):
        m_copy(d).wait_send()
    for q in range(n):
        @pl.when(z != q)
        def _():
            for h in range(g_pieces):
                g_copy(q, h, True).wait_send()


def fused(
    n, nb, allele_matrix, orthonormal_frames, segment_variances, lambda_grid, trait_levels, partition_labels, preceding_fits
):
    rows = allele_matrix.shape[0]
    blocks, width = orthonormal_frames.shape[:2]
    prot = trait_levels.shape[1]
    lams = lambda_grid.shape[0]
    old = preceding_fits[0]
    old_width = old.shape[1]
    qw = old_width * nb // n
    new_width = blocks * lams
    erows = -(-(nb * new_width + 1) // 16) * 16
    c_rows, c_cols = blocks * width, FOLDS * prot
    c_pieces = c_rows // row_piece(c_rows)
    gp = row_piece(old_width)
    g_pieces = old_width // gp
    vmem = pl.BlockSpec(memory_space=pltpu.VMEM)
    dma = pltpu.SemaphoreType.DMA
    out = pl.pallas_call(
        functools.partial(kernel, n, nb, lams),
        out_shape=(
            jax.ShapeDtypeStruct((rows, blocks * lams * prot), BF16),
            jax.ShapeDtypeStruct((old_width, qw), F32),
            jax.ShapeDtypeStruct((new_width, qw), F32),
            jax.ShapeDtypeStruct((new_width, nb * new_width), F32),
            jax.ShapeDtypeStruct((1, qw), F32),
            jax.ShapeDtypeStruct((new_width, 1), F32),
        ),
        in_specs=[vmem, vmem, vmem, pl.BlockSpec(memory_space=pltpu.SMEM), vmem, vmem, vmem],
        out_specs=(vmem,) * 6,
        scratch_shapes=[
            pltpu.VMEM((n, rows, qw), BF16),
            pltpu.VMEM((old_width, rows), BF16),
            pltpu.VMEM((blocks, rows, width), BF16),
            pltpu.VMEM((c_rows, c_cols), F32),
            pltpu.VMEM((c_rows, c_cols), BF16),
            pltpu.VMEM((c_rows, c_cols), BF16),
            pltpu.VMEM((2, c_rows, c_cols), BF16),
            pltpu.VMEM((n, old_width, qw), BF16),
            pltpu.VMEM((n, old_width, qw), BF16),
            pltpu.VMEM((n, old_width, qw), BF16),
            pltpu.VMEM((gp, qw), F32),
            pltpu.VMEM((nb, erows, rows), BF16),
            pltpu.VMEM((erows, rows), BF16),
            pltpu.VMEM((n, erows, qw + 128), F32),
            pltpu.VMEM((n, erows, qw + 128), F32),
            pltpu.VMEM((erows, qw + 128), F32),
            dma((n, nb)), dma((n,)),
            dma((2, c_pieces)), dma((2, c_pieces)),
            dma((n, g_pieces)), dma((n, g_pieces)), dma((n, g_pieces)),
            dma((nb,)), dma((nb,)), dma((n,)), dma((n,)),
        ],
        compiler_params=pltpu.CompilerParams(
            collective_id=0, has_side_effects=True, vmem_limit_bytes=56 * 1024 * 1024),
        name="ridge",
    )(allele_matrix, orthonormal_frames, segment_variances.T, lambda_grid, trait_levels, partition_labels[:, None], old)
    preds, gram_old, gram_cross, gram_new, fit_old, fit_new = out
    return (
        preds.reshape(rows, blocks, lams, prot),
        gram_old[None],
        gram_cross[None],
        gram_new[None],
        fit_old,
        fit_new.reshape(1, new_width),
    )


def segment_fitted_trait(
    projected_traits, pairwise_inner, spectral_line, lambda_grid, partition_mask_real
):
    var_width = projected_traits.shape[1]
    prot_width = pairwise_inner.shape[1] // FOLDS
    lambda_grid_size = lambda_grid.shape[0]
    pairwise_inner = pairwise_inner.reshape(var_width, FOLDS, prot_width)
    remainder = jnp.sum(pairwise_inner, axis=1, keepdims=True) - pairwise_inner
    damping_ratio = 1.0 / (spectral_line[:, None] + lambda_grid[None, :])
    ridge_coefficients = (remainder[:, :, None, :] * damping_ratio[:, None, :, None]).astype(
        jnp.bfloat16
    )
    row_count = projected_traits.shape[0]
    running_total = jnp.zeros((row_count, lambda_grid_size * prot_width), jnp.float32)
    for holdout_index in range(FOLDS):
        lookup_table = ridge_coefficients[:, holdout_index].reshape(
            var_width, lambda_grid_size * prot_width
        )
        running_total = running_total + partition_mask_real[
            :, holdout_index : holdout_index + 1
        ] * jnp.dot(projected_traits, lookup_table, preferred_element_type=jnp.float32)
    return running_total.reshape(row_count, lambda_grid_size, prot_width).astype(jnp.bfloat16)


def sum_block(local_cross):
    return lax.psum(local_cross, "smp")


def per_device(
    allele_matrix,
    orthonormal_frames,
    segment_variances,
    lambda_grid,
    trait_levels,
    partition_labels,
    preceding_fits,
):
    row_count = allele_matrix.shape[0]
    block_count = orthonormal_frames.shape[0]
    var_width = orthonormal_frames.shape[1]
    prot_width = trait_levels.shape[1]
    lambda_grid_size = lambda_grid.shape[0]
    sample_total = float(row_count * lax.axis_size("smp"))
    contract = (((0,), (0,)), ((), ()))
    member = partition_labels[:, None] == jnp.arange(FOLDS, dtype=jnp.int32)[None, :]
    partition_mask_real = member.astype(jnp.float32)
    masked = (member.astype(jnp.bfloat16)[:, :, None] * trait_levels[:, None, :]).reshape(
        row_count, FOLDS * prot_width
    )
    rotated_list = []
    local_list = []
    for entry_offset in range(block_count):
        genotype_cols = allele_matrix[:, entry_offset * var_width : (entry_offset + 1) * var_width]
        projected_traits = jnp.dot(
            genotype_cols, orthonormal_frames[entry_offset], preferred_element_type=jnp.float32
        ).astype(jnp.bfloat16)
        rotated_list.append(projected_traits)
        local_list.append(
            lax.dot_general(projected_traits, masked, contract, preferred_element_type=jnp.float32)
        )
    crossed_list = [sum_block(local_cross) for local_cross in local_list]
    pred_list = [
        segment_fitted_trait(
            rotated_list[entry_offset],
            crossed_list[entry_offset],
            segment_variances[entry_offset],
            lambda_grid,
            partition_mask_real,
        )
        for entry_offset in range(block_count)
    ]
    level0_predictions = jnp.stack(pred_list, axis=1)
    added_columns = level0_predictions[:, :, :, 0].reshape(
        row_count, block_count * lambda_grid_size
    )
    target = trait_levels[:, 0:1]
    old_cols = preceding_fits[0]
    old_width = old_cols.shape[1]
    new_width = added_columns.shape[1]
    joined = jnp.concatenate([old_cols, added_columns], axis=1)
    gathered = lax.all_gather(joined, "blk", axis=1, tiled=True)
    shard_count = gathered.shape[1] // joined.shape[1]
    pieces = gathered.reshape(row_count, shard_count, joined.shape[1])
    old_all = pieces[:, :, :old_width].reshape(row_count, shard_count * old_width)
    new_all = pieces[:, :, old_width:].reshape(row_count, shard_count * new_width)
    stacked = jnp.concatenate([old_cols, added_columns, target], axis=1)
    reduced = lax.psum_scatter(
        lax.dot_general(stacked, old_all, contract, preferred_element_type=jnp.float32),
        "smp",
        scatter_dimension=1,
        tiled=True,
    )
    gram_old = reduced[:old_width]
    gram_cross = reduced[old_width : old_width + new_width]
    fit_old = reduced[old_width + new_width :]
    right_side = jnp.concatenate([new_all, target], axis=1)
    small_gram = lax.psum(
        lax.dot_general(added_columns, right_side, contract, preferred_element_type=jnp.float32),
        "smp",
    )
    gram_new = small_gram[:, :-1]
    fit_new = small_gram[:, -1]
    return (
        level0_predictions,
        (gram_old / sample_total)[None],
        (gram_cross / sample_total)[None],
        (gram_new / sample_total)[None],
        fit_old / sample_total,
        (fit_new / sample_total)[None],
    )


def solution(mesh):
    n, nb = mesh.shape["smp"], mesh.shape["blk"]

    def program(*arrays):
        allele_matrix, frames, _, lambda_grid, _, _, preceding_fits = arrays
        old_width = preceding_fits.shape[2]
        new_width = frames.shape[0] * lambda_grid.shape[0]
        fits = (
            n % 2 == 0
            and n % nb == 0
            and (old_width * nb) % (n * 128) == 0
            and frames.shape[1] % 128 == 0
            and new_width % 8 == 0
            and nb * new_width < 128
        )
        if fits:
            return fused(n, nb, *arrays)
        return per_device(*arrays)

    placed = (
        P("smp", ("grp", "blk")),
        P(("grp", "blk"), None, None),
        P(("grp", "blk"), None),
        P(),
        P("smp", ("grp", "pen")),
        P("smp"),
        P(("grp", "pen"), "smp", "blk"),
    )
    return jax.shard_map(
        program,
        mesh=mesh,
        in_specs=placed,
        out_specs=(
            P("smp", ("grp", "blk"), None, "pen"),
            P(("grp", "pen"), "blk", "smp"),
            P(("grp", "pen"), "blk", "smp"),
            P(("grp", "pen"), "blk", None),
            P(("grp", "pen"), "smp"),
            P(("grp", "pen"), "blk"),
        ),
        check_vma=False,
    )
```

```python
import functools

import jax
import jax.numpy as jnp
from jax import lax
from jax.experimental import pallas as pl
from jax.experimental.pallas import tpu as pltpu
from jax.sharding import PartitionSpec as P

FOLDS = 4
F32 = jnp.float32
BF16 = jnp.bfloat16
MESH = pl.DeviceIdType.MESH


def row_piece(total):
    return next(size for size in (256, 128) if total % size == 0)


def kernel(
    n, nb, groups,
    allele, frames, variances, lam, trait, labels, old,
    preds_out, gram_out, small_out,
    oldq, old_t, rot, part, c_left, c_right, c_send,
    g_left, g_right, g_send, g_part, et_all, lhs, m_send, m_recv,
    x_send, x_recv, cs_send, cs_recv, gs_send, gl_recv, gr_recv,
    e_send, e_recv, ms_send, ms_recv,
):
    z = lax.axis_index("smp")
    x = lax.axis_index("blk")
    rows, old_width = old.shape
    blocks, width = frames.shape[0], frames.shape[1]
    prot = trait.shape[0]
    lams = groups
    per = n // nb
    qw = old_width // per
    c_rows = FOLDS * prot
    cp = 128
    c_pieces = blocks * c_rows // cp
    gp = row_piece(old_width)
    g_pieces = old_width // gp
    new_width = blocks * lams
    erows = et_all.shape[1]
    sample_total = float(rows * n)
    order = []
    for i in range(n // 2):
        order += [n - 1 - i, i]

    barrier = pltpu.get_barrier_semaphore()
    for d in range(1, n):
        pl.semaphore_signal(barrier, inc=1, device_id={"smp": lax.rem(z + d, n)}, device_id_type=MESH)
    for d in range(1, nb):
        pl.semaphore_signal(barrier, inc=1, device_id={"blk": lax.rem(x + d, nb)}, device_id_type=MESH)
    pl.semaphore_wait(barrier, n - 1 + nb - 1)

    def x_copy(q, d):
        cols = pl.ds(pl.multiple_of((q - x * per) * qw, qw), qw)
        return pltpu.make_async_remote_copy(
            src_ref=old.at[:, cols], dst_ref=oldq.at[q], send_sem=x_send.at[q, d], recv_sem=x_recv.at[q],
            device_id={"blk": lax.rem(x + d, nb)}, device_id_type=MESH)

    def x_wait(q):
        pltpu.make_async_remote_copy(
            src_ref=oldq.at[q], dst_ref=oldq.at[q], send_sem=x_send.at[q, 0], recv_sem=x_recv.at[q],
            device_id={"blk": lax.rem(x + 1, nb)}, device_id_type=MESH).wait_recv()

    for q in order:
        @pl.when(x == q // per)
        def _():
            for d in range(1, nb):
                x_copy(q, d).start()

    label = labels[...]
    y = trait[...]
    y_wide = y.astype(F32)
    masked = jnp.concatenate([jnp.where(label == k, y_wide, 0.0).astype(BF16) for k in range(FOLDS)], axis=0)

    def c_copy(p, right):
        piece = pl.ds(p * cp, cp)
        return pltpu.make_async_remote_copy(
            src_ref=c_send.at[0 if right else 1, piece, :],
            dst_ref=(c_left if right else c_right).at[piece, :],
            send_sem=cs_send.at[0 if right else 1, p], recv_sem=cs_recv.at[0 if right else 1, p],
            device_id={"smp": jnp.minimum(z + 1, n - 1) if right else jnp.maximum(z - 1, 0)}, device_id_type=MESH)

    for b in range(blocks):
        r = jnp.dot(allele[:, b * width:(b + 1) * width], frames[b], preferred_element_type=F32).astype(BF16)
        rot[b] = r
        part[b * c_rows:(b + 1) * c_rows, :] = jnp.dot(masked, r, preferred_element_type=F32)
        for p in range(b * c_rows // cp, (b + 1) * c_rows // cp):
            value = part[p * cp:(p + 1) * cp, :].astype(BF16)

            @pl.when(z == 0)
            def _():
                c_send[0, p * cp:(p + 1) * cp, :] = value
                c_copy(p, True).start()

            @pl.when(z == n - 1)
            def _():
                c_send[1, p * cp:(p + 1) * cp, :] = value
                c_copy(p, False).start()

    for h in range(per):
        oldq[x * per + h] = old[:, h * qw:(h + 1) * qw]
    old_t[...] = old[...].T
    def wait_for(some, who):
        for q in some:
            @pl.when(jnp.logical_and(x != q // per, who))
            def _():
                x_wait(q)

    def g_copy(q, h, right):
        piece = pl.ds(pl.multiple_of(h * gp, gp), gp)
        return pltpu.make_async_remote_copy(
            src_ref=g_send.at[q, piece, :],
            dst_ref=(g_left if right else g_right).at[q, piece, :],
            send_sem=gs_send.at[q, h], recv_sem=(gl_recv if right else gr_recv).at[q, h],
            device_id={"smp": jnp.minimum(z + 1, n - 1) if right else jnp.maximum(z - 1, 0)}, device_id_type=MESH)

    def g_piece(q, h):
        piece = pl.ds(pl.multiple_of(h * gp, gp), gp)
        g_part[...] = jnp.dot(old_t[piece, :], oldq[q], preferred_element_type=F32)

        @pl.when(z < q)
        def _():
            @pl.when(z > 0)
            def _():
                g_copy(q, h, True).wait_recv()
                g_part[...] += g_left[q, piece, :].astype(F32)
            g_send[q, piece, :] = g_part[...].astype(BF16)
            g_copy(q, h, True).start()

        @pl.when(z > q)
        def _():
            @pl.when(z < n - 1)
            def _():
                g_copy(q, h, False).wait_recv()
                g_part[...] += g_right[q, piece, :].astype(F32)
            g_send[q, piece, :] = g_part[...].astype(BF16)
            g_copy(q, h, False).start()

        @pl.when(z == q)
        def _():
            @pl.when(z > 0)
            def _():
                g_copy(q, h, True).wait_recv()
                g_part[...] += g_left[q, piece, :].astype(F32)

            @pl.when(z < n - 1)
            def _():
                g_copy(q, h, False).wait_recv()
                g_part[...] += g_right[q, piece, :].astype(F32)
            gram_out[piece, :] = g_part[...] / sample_total

    def g_group(q):
        def body(h, carry):
            g_piece(q, h)
            return carry
        lax.fori_loop(0, g_pieces, body, 0)

    in_left = z < n // 2
    is_end = jnp.logical_or(z == 0, z == n - 1)

    is_inner = jnp.logical_not(is_end)
    wait_for(order[:2], is_end)
    for i in range(n // 2):
        if i == 1:
            wait_for(order[2:], is_end)

        @pl.when(is_end)
        def _():
            g_group(jnp.where(in_left, n - 1 - i, i))

    def from_side(p, right):
        piece = slice(p * cp, (p + 1) * cp)
        has = z > 0 if right else z < n - 1
        forward = z < n - 1 if right else z > 0

        @pl.when(has)
        def _():
            c_copy(p, right).wait_recv()

            @pl.when(forward)
            def _():
                got = (c_left if right else c_right)[piece, :]
                c_send[0 if right else 1, piece, :] = (part[piece, :] + got.astype(F32)).astype(BF16)
                c_copy(p, right).start()

    for first in (True, False):
        for p in range(c_pieces):
            @pl.when(in_left)
            def _():
                from_side(p, first)

            @pl.when(jnp.logical_not(in_left))
            def _():
                from_side(p, not first)

    wait_for(order, is_inner)

    @pl.when(is_inner)
    def _():
        g_group(jnp.where(in_left, n - 1, 0))

    @pl.when(z > 0)
    def _():
        part[...] += c_left[...].astype(F32)

    @pl.when(z < n - 1)
    def _():
        part[...] += c_right[...].astype(F32)

    sel_rows = lax.broadcasted_iota(jnp.int32, (erows, lams * prot), 0)
    sel_cols = lax.broadcasted_iota(jnp.int32, (erows, lams * prot), 1)
    e0 = jnp.zeros((erows, rows), F32)
    for b in range(blocks):
        damp = [1.0 / (variances[b:b + 1, :] + lam[r]) for r in range(lams)]
        folds = [part[b * c_rows + k * prot:b * c_rows + (k + 1) * prot, :] for k in range(FOLDS)]
        total = folds[0]
        for k in range(1, FOLDS):
            total = total + folds[k]
        acc = jnp.zeros((lams * prot, rows), F32)
        for k in range(FOLDS):
            rest = total - folds[k]
            coeff = jnp.concatenate([(rest * damp[r]).astype(BF16) for r in range(lams)], axis=0)
            acc = jnp.where(
                label == k,
                lax.dot_general(coeff, rot[b], (((1,), (1,)), ((), ())), preferred_element_type=F32),
                acc)
        pred = acc.astype(BF16)
        preds_out[b * lams * prot:(b + 1) * lams * prot, :] = pred
        wanted = x * new_width + b * lams + sel_cols // prot
        sel = jnp.where(jnp.logical_and(sel_rows == wanted, sel_cols % prot == 0), 1.0, 0.0).astype(BF16)
        e0 = e0 + jnp.dot(sel, pred, preferred_element_type=F32)
    et_all[x] = e0.astype(BF16)

    def e_copy(d):
        return pltpu.make_async_remote_copy(
            src_ref=et_all.at[x], dst_ref=et_all.at[x], send_sem=e_send.at[d], recv_sem=e_recv.at[d],
            device_id={"blk": lax.rem(x + d, nb)}, device_id_type=MESH)

    def e_wait(d):
        slot = lax.rem(x + nb - d, nb)
        pltpu.make_async_remote_copy(
            src_ref=et_all.at[slot], dst_ref=et_all.at[slot], send_sem=e_send.at[d], recv_sem=e_recv.at[d],
            device_id={"blk": slot}, device_id_type=MESH).wait_recv()

    for d in range(1, nb):
        e_copy(d).start()
    t_rows = lax.broadcasted_iota(jnp.int32, (erows, prot), 0)
    t_cols = lax.broadcasted_iota(jnp.int32, (erows, prot), 1)
    t_sel = jnp.where(jnp.logical_and(t_rows == nb * new_width, t_cols == 0), 1.0, 0.0).astype(BF16)
    target = jnp.dot(t_sel, y, preferred_element_type=F32)
    lhs[...] = (e0 + target).astype(BF16)
    for q in range(n):
        m_send[q, :, :qw] = jnp.dot(lhs[...], oldq[q], preferred_element_type=F32)
    for d in range(1, nb):
        e_wait(d)
    right_side = target
    for b in range(nb):
        right_side = right_side + et_all[b].astype(F32)
    small = lax.dot_general(
        lhs[...], jnp.concatenate([right_side.astype(BF16), jnp.zeros((128 - erows, rows), BF16)], axis=0),
        (((1,), (1,)), ((), ())), preferred_element_type=F32)
    for q in range(n):
        m_send[q, :, qw:] = small

    def m_copy(d):
        return pltpu.make_async_remote_copy(
            src_ref=m_send.at[lax.rem(z + d, n)], dst_ref=m_recv.at[d], send_sem=ms_send.at[d], recv_sem=ms_recv.at[d],
            device_id={"smp": lax.rem(z + d, n)}, device_id_type=MESH)

    for d in range(1, n):
        m_copy(d).start()

    for i in range(n // 2):
        early = jnp.where(in_left, n - 1 - i, i)
        late = n - 1 - early
        if i > 0:
            @pl.when(jnp.logical_and(early != z, is_inner))
            def _():
                g_group(early)

        @pl.when(late != z)
        def _():
            g_group(late)
    g_group(z)

    total = m_send[z]
    for d in range(1, n):
        m_copy(d).wait_recv()
        total = total + m_recv[d]
    small_out[...] = total / sample_total

    for q in range(n):
        @pl.when(x == q // per)
        def _():
            for d in range(1, nb):
                x_copy(q, d).wait_send()
    for p in range(c_pieces):
        @pl.when(z < n - 1)
        def _():
            c_copy(p, True).wait_send()

        @pl.when(z > 0)
        def _():
            c_copy(p, False).wait_send()
    for d in range(1, nb):
        e_copy(d).wait_send()
    for d in range(1, n):
        m_copy(d).wait_send()
    for q in range(n):
        @pl.when(z != q)
        def _():
            for h in range(g_pieces):
                g_copy(q, h, True).wait_send()


def finish(nb, new_width, preds, gram, small, preds_out, gram_out, cross_out, new_out, fit_old_out, fit_new_out):
    preds_out[...] = preds[...]
    gram_out[0] = gram[...]
    qw = gram.shape[1]

    @pl.when(pl.program_id(0) == 0)
    def _():
        x = lax.axis_index("blk")
        mine = pl.ds(pl.multiple_of(x * new_width, 8), new_width)
        cross_out[0] = small[mine, :qw]
        new_out[0] = small[mine, qw:qw + nb * new_width]
        fit_old_out[...] = small[nb * new_width:nb * new_width + 1, :qw]
        row = small[nb * new_width:nb * new_width + 1, qw:]
        fit = row[:, :new_width]
        for b in range(1, nb):
            fit = jnp.where(x == b, row[:, b * new_width:(b + 1) * new_width], fit)
        fit_new_out[...] = fit


def fused(
    n, nb, allele_matrix, orthonormal_frames, segment_variances, lambda_grid, trait_levels, partition_labels, preceding_fits
):
    rows = allele_matrix.shape[0]
    blocks, width = orthonormal_frames.shape[:2]
    prot = trait_levels.shape[1]
    lams = lambda_grid.shape[0]
    old = preceding_fits[0]
    old_width = old.shape[1]
    qw = old_width * nb // n
    new_width = blocks * lams
    erows = -(-(nb * new_width + 1) // 16) * 16
    c_rows, c_cols = blocks * FOLDS * prot, width
    c_pieces = c_rows // 128
    gp = row_piece(old_width)
    g_pieces = old_width // gp
    vmem = pl.BlockSpec(memory_space=pltpu.VMEM)
    dma = pltpu.SemaphoreType.DMA
    out = pl.pallas_call(
        functools.partial(kernel, n, nb, lams),
        out_shape=(
            jax.ShapeDtypeStruct((blocks * lams * prot, rows), BF16),
            jax.ShapeDtypeStruct((old_width, qw), F32),
            jax.ShapeDtypeStruct((erows, qw + 128), F32),
        ),
        in_specs=[vmem, vmem, vmem, pl.BlockSpec(memory_space=pltpu.SMEM), vmem, vmem, vmem],
        out_specs=(vmem,) * 3,
        scratch_shapes=[
            pltpu.VMEM((n, rows, qw), BF16),
            pltpu.VMEM((old_width, rows), BF16),
            pltpu.VMEM((blocks, rows, width), BF16),
            pltpu.VMEM((c_rows, c_cols), F32),
            pltpu.VMEM((c_rows, c_cols), BF16),
            pltpu.VMEM((c_rows, c_cols), BF16),
            pltpu.VMEM((2, c_rows, c_cols), BF16),
            pltpu.VMEM((n, old_width, qw), BF16),
            pltpu.VMEM((n, old_width, qw), BF16),
            pltpu.VMEM((n, old_width, qw), BF16),
            pltpu.VMEM((gp, qw), F32),
            pltpu.VMEM((nb, erows, rows), BF16),
            pltpu.VMEM((erows, rows), BF16),
            pltpu.VMEM((n, erows, qw + 128), F32),
            pltpu.VMEM((n, erows, qw + 128), F32),
            dma((n, nb)), dma((n,)),
            dma((2, c_pieces)), dma((2, c_pieces)),
            dma((n, g_pieces)), dma((n, g_pieces)), dma((n, g_pieces)),
            dma((nb,)), dma((nb,)), dma((n,)), dma((n,)),
        ],
        compiler_params=pltpu.CompilerParams(
            collective_id=0, has_side_effects=True, vmem_limit_bytes=56 * 1024 * 1024),
        name="ridge",
    )(allele_matrix, orthonormal_frames, segment_variances, lambda_grid, trait_levels.T, partition_labels[None], old)
    steps = 4
    p_rows, g_rows = out[0].shape[0] // steps, old_width // steps
    whole = lambda *shape: pl.BlockSpec(shape, lambda i: (0,) * len(shape))
    preds, gram_old, gram_cross, gram_new, fit_old, fit_new = pl.pallas_call(
        functools.partial(finish, nb, new_width),
        grid=(steps,),
        out_shape=(
            jax.ShapeDtypeStruct(out[0].shape, BF16),
            jax.ShapeDtypeStruct((1, old_width, qw), F32),
            jax.ShapeDtypeStruct((1, new_width, qw), F32),
            jax.ShapeDtypeStruct((1, new_width, nb * new_width), F32),
            jax.ShapeDtypeStruct((1, qw), F32),
            jax.ShapeDtypeStruct((1, new_width), F32),
        ),
        in_specs=[
            pl.BlockSpec((p_rows, rows), lambda i: (i, 0)),
            pl.BlockSpec((g_rows, qw), lambda i: (i, 0)),
            whole(erows, qw + 128),
        ],
        out_specs=(
            pl.BlockSpec((p_rows, rows), lambda i: (i, 0)),
            pl.BlockSpec((1, g_rows, qw), lambda i: (0, i, 0)),
            whole(1, new_width, qw),
            whole(1, new_width, nb * new_width),
            whole(1, qw),
            whole(1, new_width),
        ),
        name="finish",
    )(*out)
    preds = preds.reshape(blocks, lams, prot, rows).transpose(3, 0, 1, 2)
    return preds, gram_old, gram_cross, gram_new, fit_old, fit_new


def segment_fitted_trait(
    projected_traits, pairwise_inner, spectral_line, lambda_grid, partition_mask_real
):
    var_width = projected_traits.shape[1]
    prot_width = pairwise_inner.shape[1] // FOLDS
    lambda_grid_size = lambda_grid.shape[0]
    pairwise_inner = pairwise_inner.reshape(var_width, FOLDS, prot_width)
    remainder = jnp.sum(pairwise_inner, axis=1, keepdims=True) - pairwise_inner
    damping_ratio = 1.0 / (spectral_line[:, None] + lambda_grid[None, :])
    ridge_coefficients = (remainder[:, :, None, :] * damping_ratio[:, None, :, None]).astype(
        jnp.bfloat16
    )
    row_count = projected_traits.shape[0]
    running_total = jnp.zeros((row_count, lambda_grid_size * prot_width), jnp.float32)
    for holdout_index in range(FOLDS):
        lookup_table = ridge_coefficients[:, holdout_index].reshape(
            var_width, lambda_grid_size * prot_width
        )
        running_total = running_total + partition_mask_real[
            :, holdout_index : holdout_index + 1
        ] * jnp.dot(projected_traits, lookup_table, preferred_element_type=jnp.float32)
    return running_total.reshape(row_count, lambda_grid_size, prot_width).astype(jnp.bfloat16)


def sum_block(local_cross):
    return lax.psum(local_cross, "smp")


def per_device(
    allele_matrix,
    orthonormal_frames,
    segment_variances,
    lambda_grid,
    trait_levels,
    partition_labels,
    preceding_fits,
):
    row_count = allele_matrix.shape[0]
    block_count = orthonormal_frames.shape[0]
    var_width = orthonormal_frames.shape[1]
    prot_width = trait_levels.shape[1]
    lambda_grid_size = lambda_grid.shape[0]
    sample_total = float(row_count * lax.axis_size("smp"))
    contract = (((0,), (0,)), ((), ()))
    member = partition_labels[:, None] == jnp.arange(FOLDS, dtype=jnp.int32)[None, :]
    partition_mask_real = member.astype(jnp.float32)
    masked = (member.astype(jnp.bfloat16)[:, :, None] * trait_levels[:, None, :]).reshape(
        row_count, FOLDS * prot_width
    )
    rotated_list = []
    local_list = []
    for entry_offset in range(block_count):
        genotype_cols = allele_matrix[:, entry_offset * var_width : (entry_offset + 1) * var_width]
        projected_traits = jnp.dot(
            genotype_cols, orthonormal_frames[entry_offset], preferred_element_type=jnp.float32
        ).astype(jnp.bfloat16)
        rotated_list.append(projected_traits)
        local_list.append(
            lax.dot_general(projected_traits, masked, contract, preferred_element_type=jnp.float32)
        )
    crossed_list = [sum_block(local_cross) for local_cross in local_list]
    pred_list = [
        segment_fitted_trait(
            rotated_list[entry_offset],
            crossed_list[entry_offset],
            segment_variances[entry_offset],
            lambda_grid,
            partition_mask_real,
        )
        for entry_offset in range(block_count)
    ]
    level0_predictions = jnp.stack(pred_list, axis=1)
    added_columns = level0_predictions[:, :, :, 0].reshape(
        row_count, block_count * lambda_grid_size
    )
    target = trait_levels[:, 0:1]
    old_cols = preceding_fits[0]
    old_width = old_cols.shape[1]
    new_width = added_columns.shape[1]
    joined = jnp.concatenate([old_cols, added_columns], axis=1)
    gathered = lax.all_gather(joined, "blk", axis=1, tiled=True)
    shard_count = gathered.shape[1] // joined.shape[1]
    pieces = gathered.reshape(row_count, shard_count, joined.shape[1])
    old_all = pieces[:, :, :old_width].reshape(row_count, shard_count * old_width)
    new_all = pieces[:, :, old_width:].reshape(row_count, shard_count * new_width)
    stacked = jnp.concatenate([old_cols, added_columns, target], axis=1)
    reduced = lax.psum_scatter(
        lax.dot_general(stacked, old_all, contract, preferred_element_type=jnp.float32),
        "smp",
        scatter_dimension=1,
        tiled=True,
    )
    gram_old = reduced[:old_width]
    gram_cross = reduced[old_width : old_width + new_width]
    fit_old = reduced[old_width + new_width :]
    right_side = jnp.concatenate([new_all, target], axis=1)
    small_gram = lax.psum(
        lax.dot_general(added_columns, right_side, contract, preferred_element_type=jnp.float32),
        "smp",
    )
    gram_new = small_gram[:, :-1]
    fit_new = small_gram[:, -1]
    return (
        level0_predictions,
        (gram_old / sample_total)[None],
        (gram_cross / sample_total)[None],
        (gram_new / sample_total)[None],
        fit_old / sample_total,
        (fit_new / sample_total)[None],
    )


def solution(mesh):
    n, nb = mesh.shape["smp"], mesh.shape["blk"]

    def program(*arrays):
        _, frames, _, lambda_grid, trait_levels, _, preceding_fits = arrays
        old_width = preceding_fits.shape[2]
        new_width = frames.shape[0] * lambda_grid.shape[0]
        fits = (
            n % 2 == 0
            and n % nb == 0
            and (old_width * nb) % (n * 128) == 0
            and frames.shape[1] % 128 == 0
            and new_width % 8 == 0
            and old_width % 64 == 0
            and FOLDS * trait_levels.shape[1] % 128 == 0
            and nb * new_width < 128
        )
        if fits:
            return fused(n, nb, *arrays)
        return per_device(*arrays)

    placed = (
        P("smp", ("grp", "blk")),
        P(("grp", "blk"), None, None),
        P(("grp", "blk"), None),
        P(),
        P("smp", ("grp", "pen")),
        P("smp"),
        P(("grp", "pen"), "smp", "blk"),
    )
    return jax.shard_map(
        program,
        mesh=mesh,
        in_specs=placed,
        out_specs=(
            P("smp", ("grp", "blk"), None, "pen"),
            P(("grp", "pen"), "blk", "smp"),
            P(("grp", "pen"), "blk", "smp"),
            P(("grp", "pen"), "blk", None),
            P(("grp", "pen"), "smp"),
            P(("grp", "pen"), "blk"),
        ),
        check_vma=False,
    )
```

```python
import functools

import jax
import jax.numpy as jnp
from jax import lax
from jax.experimental import pallas as pl
from jax.experimental.pallas import tpu as pltpu
from jax.sharding import PartitionSpec as P

FOLDS = 4
F32 = jnp.float32
BF16 = jnp.bfloat16
MESH = pl.DeviceIdType.MESH


def row_piece(total):
    return next(size for size in (256, 128) if total % size == 0)


def kernel(
    n, nb, groups,
    allele_in, frames_in, variances, lam, trait, labels, old_in,
    preds_out, gram_out, small_out,
    allele, frames, old, preds, gram, in_sem, out_sem, gram_sem,
    oldq, old_t, rot, part, c_left, c_right, c_send,
    g_left, g_right, g_send, g_part, et_all, lhs, m_send, m_recv,
    x_send, x_recv, cs_send, cs_recv, gs_send, gl_recv, gr_recv,
    e_send, e_recv, ms_send, ms_recv,
):
    z = lax.axis_index("smp")
    x = lax.axis_index("blk")
    rows, old_width = old.shape
    blocks, width = frames.shape[0], frames.shape[1]
    prot = trait.shape[0]
    lams = groups
    per = n // nb
    qw = old_width // per
    c_rows = FOLDS * prot
    cp = 128
    c_pieces = blocks * c_rows // cp
    gp = row_piece(old_width)
    g_pieces = old_width // gp
    new_width = blocks * lams
    erows = et_all.shape[1]
    sample_total = float(rows * n)
    order = []
    for i in range(n // 2):
        order += [n - 1 - i, i]

    loads = [
        pltpu.make_async_copy(source, place, in_sem.at[i])
        for i, (source, place) in enumerate(((allele_in, allele), (frames_in, frames), (old_in, old)))
    ]
    for load in loads:
        load.start()
    barrier = pltpu.get_barrier_semaphore()
    for d in range(1, n):
        pl.semaphore_signal(barrier, inc=1, device_id={"smp": lax.rem(z + d, n)}, device_id_type=MESH)
    for d in range(1, nb):
        pl.semaphore_signal(barrier, inc=1, device_id={"blk": lax.rem(x + d, nb)}, device_id_type=MESH)
    pl.semaphore_wait(barrier, n - 1 + nb - 1)

    def x_copy(q, d):
        cols = pl.ds(pl.multiple_of((q - x * per) * qw, qw), qw)
        return pltpu.make_async_remote_copy(
            src_ref=old_in.at[:, cols], dst_ref=oldq.at[q], send_sem=x_send.at[q, d], recv_sem=x_recv.at[q],
            device_id={"blk": lax.rem(x + d, nb)}, device_id_type=MESH)

    def x_wait(q):
        pltpu.make_async_remote_copy(
            src_ref=oldq.at[q], dst_ref=oldq.at[q], send_sem=x_send.at[q, 0], recv_sem=x_recv.at[q],
            device_id={"blk": lax.rem(x + 1, nb)}, device_id_type=MESH).wait_recv()

    for q in order:
        @pl.when(x == q // per)
        def _():
            for d in range(1, nb):
                x_copy(q, d).start()

    label = labels[...]
    y = trait[...]
    y_wide = y.astype(F32)
    masked = jnp.concatenate([jnp.where(label == k, y_wide, 0.0).astype(BF16) for k in range(FOLDS)], axis=0)

    def c_copy(p, right):
        piece = pl.ds(p * cp, cp)
        return pltpu.make_async_remote_copy(
            src_ref=c_send.at[0 if right else 1, piece, :],
            dst_ref=(c_left if right else c_right).at[piece, :],
            send_sem=cs_send.at[0 if right else 1, p], recv_sem=cs_recv.at[0 if right else 1, p],
            device_id={"smp": jnp.minimum(z + 1, n - 1) if right else jnp.maximum(z - 1, 0)}, device_id_type=MESH)

    loads[0].wait()
    loads[1].wait()
    for b in range(blocks):
        r = jnp.dot(allele[:, b * width:(b + 1) * width], frames[b], preferred_element_type=F32).astype(BF16)
        rot[b] = r
        part[b * c_rows:(b + 1) * c_rows, :] = jnp.dot(masked, r, preferred_element_type=F32)
        for p in range(b * c_rows // cp, (b + 1) * c_rows // cp):
            value = part[p * cp:(p + 1) * cp, :].astype(BF16)

            @pl.when(z == 0)
            def _():
                c_send[0, p * cp:(p + 1) * cp, :] = value
                c_copy(p, True).start()

            @pl.when(z == n - 1)
            def _():
                c_send[1, p * cp:(p + 1) * cp, :] = value
                c_copy(p, False).start()

    loads[2].wait()
    for h in range(per):
        oldq[x * per + h] = old[:, h * qw:(h + 1) * qw]
    old_t[...] = old[...].T
    def wait_for(some, who):
        for q in some:
            @pl.when(jnp.logical_and(x != q // per, who))
            def _():
                x_wait(q)

    def g_copy(q, h, right):
        piece = pl.ds(pl.multiple_of(h * gp, gp), gp)
        return pltpu.make_async_remote_copy(
            src_ref=g_send.at[q, piece, :],
            dst_ref=(g_left if right else g_right).at[q, piece, :],
            send_sem=gs_send.at[q, h], recv_sem=(gl_recv if right else gr_recv).at[q, h],
            device_id={"smp": jnp.minimum(z + 1, n - 1) if right else jnp.maximum(z - 1, 0)}, device_id_type=MESH)

    def gram_copy(h):
        piece = pl.ds(pl.multiple_of(h * gp, gp), gp)
        return pltpu.make_async_copy(gram.at[piece, :], gram_out.at[piece, :], gram_sem.at[h])

    def g_piece(q, h):
        piece = pl.ds(pl.multiple_of(h * gp, gp), gp)
        g_part[...] = jnp.dot(old_t[piece, :], oldq[q], preferred_element_type=F32)

        @pl.when(z < q)
        def _():
            @pl.when(z > 0)
            def _():
                g_copy(q, h, True).wait_recv()
                g_part[...] += g_left[q, piece, :].astype(F32)
            g_send[q, piece, :] = g_part[...].astype(BF16)
            g_copy(q, h, True).start()

        @pl.when(z > q)
        def _():
            @pl.when(z < n - 1)
            def _():
                g_copy(q, h, False).wait_recv()
                g_part[...] += g_right[q, piece, :].astype(F32)
            g_send[q, piece, :] = g_part[...].astype(BF16)
            g_copy(q, h, False).start()

        @pl.when(z == q)
        def _():
            @pl.when(z > 0)
            def _():
                g_copy(q, h, True).wait_recv()
                g_part[...] += g_left[q, piece, :].astype(F32)

            @pl.when(z < n - 1)
            def _():
                g_copy(q, h, False).wait_recv()
                g_part[...] += g_right[q, piece, :].astype(F32)
            gram[piece, :] = g_part[...] / sample_total
            gram_copy(h).start()

    def g_group(q):
        def body(h, carry):
            g_piece(q, h)
            return carry
        lax.fori_loop(0, g_pieces, body, 0)

    in_left = z < n // 2
    is_end = jnp.logical_or(z == 0, z == n - 1)

    is_inner = jnp.logical_not(is_end)
    wait_for(order[:2], is_end)
    for i in range(n // 2):
        if i == 1:
            wait_for(order[2:], is_end)

        @pl.when(is_end)
        def _():
            g_group(jnp.where(in_left, n - 1 - i, i))

    def from_side(p, right):
        piece = slice(p * cp, (p + 1) * cp)
        has = z > 0 if right else z < n - 1
        forward = z < n - 1 if right else z > 0

        @pl.when(has)
        def _():
            c_copy(p, right).wait_recv()

            @pl.when(forward)
            def _():
                got = (c_left if right else c_right)[piece, :]
                c_send[0 if right else 1, piece, :] = (part[piece, :] + got.astype(F32)).astype(BF16)
                c_copy(p, right).start()

    for first in (True, False):
        for p in range(c_pieces):
            @pl.when(in_left)
            def _():
                from_side(p, first)

            @pl.when(jnp.logical_not(in_left))
            def _():
                from_side(p, not first)

    wait_for(order, is_inner)

    @pl.when(is_inner)
    def _():
        g_group(jnp.where(in_left, n - 1, 0))

    @pl.when(z > 0)
    def _():
        part[...] += c_left[...].astype(F32)

    @pl.when(z < n - 1)
    def _():
        part[...] += c_right[...].astype(F32)

    sel_rows = lax.broadcasted_iota(jnp.int32, (erows, lams * prot), 0)
    sel_cols = lax.broadcasted_iota(jnp.int32, (erows, lams * prot), 1)
    e0 = jnp.zeros((erows, rows), F32)
    for b in range(blocks):
        damp = [1.0 / (variances[b:b + 1, :] + lam[r]) for r in range(lams)]
        folds = [part[b * c_rows + k * prot:b * c_rows + (k + 1) * prot, :] for k in range(FOLDS)]
        total = folds[0]
        for k in range(1, FOLDS):
            total = total + folds[k]
        acc = jnp.zeros((lams * prot, rows), F32)
        for k in range(FOLDS):
            rest = total - folds[k]
            coeff = jnp.concatenate([(rest * damp[r]).astype(BF16) for r in range(lams)], axis=0)
            acc = jnp.where(
                label == k,
                lax.dot_general(coeff, rot[b], (((1,), (1,)), ((), ())), preferred_element_type=F32),
                acc)
        pred = acc.astype(BF16)
        preds[b * lams * prot:(b + 1) * lams * prot, :] = pred
        wanted = x * new_width + b * lams + sel_cols // prot
        sel = jnp.where(jnp.logical_and(sel_rows == wanted, sel_cols % prot == 0), 1.0, 0.0).astype(BF16)
        e0 = e0 + jnp.dot(sel, pred, preferred_element_type=F32)
    preds_copy = pltpu.make_async_copy(preds, preds_out, out_sem)
    preds_copy.start()
    et_all[x] = e0.astype(BF16)

    def e_copy(d):
        return pltpu.make_async_remote_copy(
            src_ref=et_all.at[x], dst_ref=et_all.at[x], send_sem=e_send.at[d], recv_sem=e_recv.at[d],
            device_id={"blk": lax.rem(x + d, nb)}, device_id_type=MESH)

    def e_wait(d):
        slot = lax.rem(x + nb - d, nb)
        pltpu.make_async_remote_copy(
            src_ref=et_all.at[slot], dst_ref=et_all.at[slot], send_sem=e_send.at[d], recv_sem=e_recv.at[d],
            device_id={"blk": slot}, device_id_type=MESH).wait_recv()

    for d in range(1, nb):
        e_copy(d).start()
    t_rows = lax.broadcasted_iota(jnp.int32, (erows, prot), 0)
    t_cols = lax.broadcasted_iota(jnp.int32, (erows, prot), 1)
    t_sel = jnp.where(jnp.logical_and(t_rows == nb * new_width, t_cols == 0), 1.0, 0.0).astype(BF16)
    target = jnp.dot(t_sel, y, preferred_element_type=F32)
    lhs[...] = (e0 + target).astype(BF16)
    for q in range(n):
        m_send[q, :, :qw] = jnp.dot(lhs[...], oldq[q], preferred_element_type=F32)
    for d in range(1, nb):
        e_wait(d)
    right_side = target
    for b in range(nb):
        right_side = right_side + et_all[b].astype(F32)
    small = lax.dot_general(
        lhs[...], jnp.concatenate([right_side.astype(BF16), jnp.zeros((128 - erows, rows), BF16)], axis=0),
        (((1,), (1,)), ((), ())), preferred_element_type=F32)
    for q in range(n):
        m_send[q, :, qw:] = small

    def m_copy(d):
        return pltpu.make_async_remote_copy(
            src_ref=m_send.at[lax.rem(z + d, n)], dst_ref=m_recv.at[d], send_sem=ms_send.at[d], recv_sem=ms_recv.at[d],
            device_id={"smp": lax.rem(z + d, n)}, device_id_type=MESH)

    for d in range(1, n):
        m_copy(d).start()

    for i in range(n // 2):
        early = jnp.where(in_left, n - 1 - i, i)
        late = n - 1 - early
        if i > 0:
            @pl.when(jnp.logical_and(early != z, is_inner))
            def _():
                g_group(early)

        @pl.when(late != z)
        def _():
            g_group(late)
    g_group(z)

    total = m_send[z]
    for d in range(1, n):
        m_copy(d).wait_recv()
        total = total + m_recv[d]
    small_out[...] = total / sample_total

    preds_copy.wait()
    for h in range(g_pieces):
        gram_copy(h).wait()
    for q in range(n):
        @pl.when(x == q // per)
        def _():
            for d in range(1, nb):
                x_copy(q, d).wait_send()
    for p in range(c_pieces):
        @pl.when(z < n - 1)
        def _():
            c_copy(p, True).wait_send()

        @pl.when(z > 0)
        def _():
            c_copy(p, False).wait_send()
    for d in range(1, nb):
        e_copy(d).wait_send()
    for d in range(1, n):
        m_copy(d).wait_send()
    for q in range(n):
        @pl.when(z != q)
        def _():
            for h in range(g_pieces):
                g_copy(q, h, True).wait_send()


def finish(
    nb, new_width, preds_in, gram_in, small, preds_out, gram_out, cross_out, new_out, fit_old_out, fit_new_out,
    preds, gram, in_sem, out_sem
):
    steps = in_sem.shape[0] // 2
    moves = []
    for i in range(steps):
        for k, (source, place, end) in enumerate(((gram_in, gram, gram_out.at[0]), (preds_in, preds, preds_out))):
            size = source.shape[0] // steps
            piece = pl.ds(i * size, size)
            moves.append((
                pltpu.make_async_copy(source.at[piece, :], place.at[piece, :], in_sem.at[2 * i + k]),
                pltpu.make_async_copy(place.at[piece, :], end.at[piece, :], out_sem.at[2 * i + k]),
            ))
    for load, _ in moves:
        load.start()
    qw = gram.shape[1]
    x = lax.axis_index("blk")
    mine = pl.ds(pl.multiple_of(x * new_width, 8), new_width)
    cross_out[0] = small[mine, :qw]
    new_out[0] = small[mine, qw:qw + nb * new_width]
    fit_old_out[...] = small[nb * new_width:nb * new_width + 1, :qw]
    row = small[nb * new_width:nb * new_width + 1, qw:]
    fit = row[:, :new_width]
    for b in range(1, nb):
        fit = jnp.where(x == b, row[:, b * new_width:(b + 1) * new_width], fit)
    fit_new_out[...] = fit
    for load, store in moves:
        load.wait()
        store.start()
    for _, store in moves:
        store.wait()


def fused(
    n, nb, allele_matrix, orthonormal_frames, segment_variances, lambda_grid, trait_levels, partition_labels, preceding_fits
):
    rows = allele_matrix.shape[0]
    blocks, width = orthonormal_frames.shape[:2]
    prot = trait_levels.shape[1]
    lams = lambda_grid.shape[0]
    old = preceding_fits[0]
    old_width = old.shape[1]
    qw = old_width * nb // n
    new_width = blocks * lams
    erows = -(-(nb * new_width + 1) // 16) * 16
    c_rows, c_cols = blocks * FOLDS * prot, width
    c_pieces = c_rows // 128
    gp = row_piece(old_width)
    g_pieces = old_width // gp
    vmem = pl.BlockSpec(memory_space=pltpu.VMEM)
    hbm = pl.BlockSpec(memory_space=pl.ANY)
    dma = pltpu.SemaphoreType.DMA
    out = pl.pallas_call(
        functools.partial(kernel, n, nb, lams),
        out_shape=(
            jax.ShapeDtypeStruct((blocks * lams * prot, rows), BF16),
            jax.ShapeDtypeStruct((old_width, qw), F32),
            jax.ShapeDtypeStruct((erows, qw + 128), F32),
        ),
        in_specs=[hbm, hbm, vmem, pl.BlockSpec(memory_space=pltpu.SMEM), vmem, vmem, hbm],
        out_specs=(hbm, hbm, vmem),
        scratch_shapes=[
            pltpu.VMEM(allele_matrix.shape, BF16),
            pltpu.VMEM(orthonormal_frames.shape, BF16),
            pltpu.VMEM(old.shape, BF16),
            pltpu.VMEM((blocks * lams * prot, rows), BF16),
            pltpu.VMEM((old_width, qw), F32),
            dma((3,)), dma, dma((g_pieces,)),
            pltpu.VMEM((n, rows, qw), BF16),
            pltpu.VMEM((old_width, rows), BF16),
            pltpu.VMEM((blocks, rows, width), BF16),
            pltpu.VMEM((c_rows, c_cols), F32),
            pltpu.VMEM((c_rows, c_cols), BF16),
            pltpu.VMEM((c_rows, c_cols), BF16),
            pltpu.VMEM((2, c_rows, c_cols), BF16),
            pltpu.VMEM((n, old_width, qw), BF16),
            pltpu.VMEM((n, old_width, qw), BF16),
            pltpu.VMEM((n, old_width, qw), BF16),
            pltpu.VMEM((gp, qw), F32),
            pltpu.VMEM((nb, erows, rows), BF16),
            pltpu.VMEM((erows, rows), BF16),
            pltpu.VMEM((n, erows, qw + 128), F32),
            pltpu.VMEM((n, erows, qw + 128), F32),
            dma((n, nb)), dma((n,)),
            dma((2, c_pieces)), dma((2, c_pieces)),
            dma((n, g_pieces)), dma((n, g_pieces)), dma((n, g_pieces)),
            dma((nb,)), dma((nb,)), dma((n,)), dma((n,)),
        ],
        compiler_params=pltpu.CompilerParams(
            collective_id=0, has_side_effects=True, vmem_limit_bytes=56 * 1024 * 1024),
        name="ridge",
    )(allele_matrix, orthonormal_frames, segment_variances, lambda_grid, trait_levels.T, partition_labels[None], old)
    steps = 4
    preds, gram_old, gram_cross, gram_new, fit_old, fit_new = pl.pallas_call(
        functools.partial(finish, nb, new_width),
        out_shape=(
            jax.ShapeDtypeStruct(out[0].shape, BF16),
            jax.ShapeDtypeStruct((1, old_width, qw), F32),
            jax.ShapeDtypeStruct((1, new_width, qw), F32),
            jax.ShapeDtypeStruct((1, new_width, nb * new_width), F32),
            jax.ShapeDtypeStruct((1, qw), F32),
            jax.ShapeDtypeStruct((1, new_width), F32),
        ),
        in_specs=[hbm, hbm, vmem],
        out_specs=(hbm, hbm, vmem, vmem, vmem, vmem),
        scratch_shapes=[
            pltpu.VMEM(out[0].shape, BF16),
            pltpu.VMEM(out[1].shape, F32),
            dma((2 * steps,)), dma((2 * steps,)),
        ],
        compiler_params=pltpu.CompilerParams(vmem_limit_bytes=56 * 1024 * 1024),
        name="finish",
    )(*out)
    preds = preds.reshape(blocks, lams, prot, rows).transpose(3, 0, 1, 2)
    return preds, gram_old, gram_cross, gram_new, fit_old, fit_new


def segment_fitted_trait(
    projected_traits, pairwise_inner, spectral_line, lambda_grid, partition_mask_real
):
    var_width = projected_traits.shape[1]
    prot_width = pairwise_inner.shape[1] // FOLDS
    lambda_grid_size = lambda_grid.shape[0]
    pairwise_inner = pairwise_inner.reshape(var_width, FOLDS, prot_width)
    remainder = jnp.sum(pairwise_inner, axis=1, keepdims=True) - pairwise_inner
    damping_ratio = 1.0 / (spectral_line[:, None] + lambda_grid[None, :])
    ridge_coefficients = (remainder[:, :, None, :] * damping_ratio[:, None, :, None]).astype(
        jnp.bfloat16
    )
    row_count = projected_traits.shape[0]
    running_total = jnp.zeros((row_count, lambda_grid_size * prot_width), jnp.float32)
    for holdout_index in range(FOLDS):
        lookup_table = ridge_coefficients[:, holdout_index].reshape(
            var_width, lambda_grid_size * prot_width
        )
        running_total = running_total + partition_mask_real[
            :, holdout_index : holdout_index + 1
        ] * jnp.dot(projected_traits, lookup_table, preferred_element_type=jnp.float32)
    return running_total.reshape(row_count, lambda_grid_size, prot_width).astype(jnp.bfloat16)


def sum_block(local_cross):
    return lax.psum(local_cross, "smp")


def per_device(
    allele_matrix,
    orthonormal_frames,
    segment_variances,
    lambda_grid,
    trait_levels,
    partition_labels,
    preceding_fits,
):
    row_count = allele_matrix.shape[0]
    block_count = orthonormal_frames.shape[0]
    var_width = orthonormal_frames.shape[1]
    prot_width = trait_levels.shape[1]
    lambda_grid_size = lambda_grid.shape[0]
    sample_total = float(row_count * lax.axis_size("smp"))
    contract = (((0,), (0,)), ((), ()))
    member = partition_labels[:, None] == jnp.arange(FOLDS, dtype=jnp.int32)[None, :]
    partition_mask_real = member.astype(jnp.float32)
    masked = (member.astype(jnp.bfloat16)[:, :, None] * trait_levels[:, None, :]).reshape(
        row_count, FOLDS * prot_width
    )
    rotated_list = []
    local_list = []
    for entry_offset in range(block_count):
        genotype_cols = allele_matrix[:, entry_offset * var_width : (entry_offset + 1) * var_width]
        projected_traits = jnp.dot(
            genotype_cols, orthonormal_frames[entry_offset], preferred_element_type=jnp.float32
        ).astype(jnp.bfloat16)
        rotated_list.append(projected_traits)
        local_list.append(
            lax.dot_general(projected_traits, masked, contract, preferred_element_type=jnp.float32)
        )
    crossed_list = [sum_block(local_cross) for local_cross in local_list]
    pred_list = [
        segment_fitted_trait(
            rotated_list[entry_offset],
            crossed_list[entry_offset],
            segment_variances[entry_offset],
            lambda_grid,
            partition_mask_real,
        )
        for entry_offset in range(block_count)
    ]
    level0_predictions = jnp.stack(pred_list, axis=1)
    added_columns = level0_predictions[:, :, :, 0].reshape(
        row_count, block_count * lambda_grid_size
    )
    target = trait_levels[:, 0:1]
    old_cols = preceding_fits[0]
    old_width = old_cols.shape[1]
    new_width = added_columns.shape[1]
    joined = jnp.concatenate([old_cols, added_columns], axis=1)
    gathered = lax.all_gather(joined, "blk", axis=1, tiled=True)
    shard_count = gathered.shape[1] // joined.shape[1]
    pieces = gathered.reshape(row_count, shard_count, joined.shape[1])
    old_all = pieces[:, :, :old_width].reshape(row_count, shard_count * old_width)
    new_all = pieces[:, :, old_width:].reshape(row_count, shard_count * new_width)
    stacked = jnp.concatenate([old_cols, added_columns, target], axis=1)
    reduced = lax.psum_scatter(
        lax.dot_general(stacked, old_all, contract, preferred_element_type=jnp.float32),
        "smp",
        scatter_dimension=1,
        tiled=True,
    )
    gram_old = reduced[:old_width]
    gram_cross = reduced[old_width : old_width + new_width]
    fit_old = reduced[old_width + new_width :]
    right_side = jnp.concatenate([new_all, target], axis=1)
    small_gram = lax.psum(
        lax.dot_general(added_columns, right_side, contract, preferred_element_type=jnp.float32),
        "smp",
    )
    gram_new = small_gram[:, :-1]
    fit_new = small_gram[:, -1]
    return (
        level0_predictions,
        (gram_old / sample_total)[None],
        (gram_cross / sample_total)[None],
        (gram_new / sample_total)[None],
        fit_old / sample_total,
        (fit_new / sample_total)[None],
    )


def solution(mesh):
    n, nb = mesh.shape["smp"], mesh.shape["blk"]

    def program(*arrays):
        _, frames, _, lambda_grid, trait_levels, _, preceding_fits = arrays
        old_width = preceding_fits.shape[2]
        new_width = frames.shape[0] * lambda_grid.shape[0]
        fits = (
            n % 2 == 0
            and n % nb == 0
            and (old_width * nb) % (n * 128) == 0
            and frames.shape[1] % 128 == 0
            and new_width % 8 == 0
            and old_width % 64 == 0
            and FOLDS * trait_levels.shape[1] % 128 == 0
            and nb * new_width < 128
        )
        if fits:
            return fused(n, nb, *arrays)
        return per_device(*arrays)

    placed = (
        P("smp", ("grp", "blk")),
        P(("grp", "blk"), None, None),
        P(("grp", "blk"), None),
        P(),
        P("smp", ("grp", "pen")),
        P("smp"),
        P(("grp", "pen"), "smp", "blk"),
    )
    return jax.shard_map(
        program,
        mesh=mesh,
        in_specs=placed,
        out_specs=(
            P("smp", ("grp", "blk"), None, "pen"),
            P(("grp", "pen"), "blk", "smp"),
            P(("grp", "pen"), "blk", "smp"),
            P(("grp", "pen"), "blk", None),
            P(("grp", "pen"), "smp"),
            P(("grp", "pen"), "blk"),
        ),
        check_vma=False,
    )
```

```python
import functools

import jax
import jax.numpy as jnp
from jax import lax
from jax.experimental import pallas as pl
from jax.experimental.pallas import tpu as pltpu
from jax.sharding import PartitionSpec as P

FOLDS = 4
F32 = jnp.float32
BF16 = jnp.bfloat16
MESH = pl.DeviceIdType.MESH


def row_piece(total):
    return next(size for size in (256, 128) if total % size == 0)


def kernel(
    n, nb, groups,
    allele, frames, variances, lam, trait, labels, old,
    preds_out, gram_out, small_out,
    preds, gram, out_sem, gram_sem,
    oldq, old_t, rot, part, c_left, c_right, c_send,
    g_left, g_right, g_send, g_part, et_all, lhs, m_send, m_recv,
    x_send, x_recv, cs_send, cs_recv, gs_send, gl_recv, gr_recv,
    e_send, e_recv, ms_send, ms_recv,
):
    z = lax.axis_index("smp")
    x = lax.axis_index("blk")
    rows, old_width = old.shape
    blocks, width = frames.shape[0], frames.shape[1]
    prot = trait.shape[0]
    lams = groups
    per = n // nb
    qw = old_width // per
    c_rows = FOLDS * prot
    cp = 128
    c_pieces = blocks * c_rows // cp
    gp = row_piece(old_width)
    g_pieces = old_width // gp
    new_width = blocks * lams
    erows = et_all.shape[1]
    sample_total = float(rows * n)
    order = []
    for i in range(n // 2):
        order += [n - 1 - i, i]

    barrier = pltpu.get_barrier_semaphore()
    for d in range(1, n):
        pl.semaphore_signal(barrier, inc=1, device_id={"smp": lax.rem(z + d, n)}, device_id_type=MESH)
    for d in range(1, nb):
        pl.semaphore_signal(barrier, inc=1, device_id={"blk": lax.rem(x + d, nb)}, device_id_type=MESH)
    pl.semaphore_wait(barrier, n - 1 + nb - 1)

    def x_copy(q, d):
        cols = pl.ds(pl.multiple_of((q - x * per) * qw, qw), qw)
        return pltpu.make_async_remote_copy(
            src_ref=old.at[:, cols], dst_ref=oldq.at[q], send_sem=x_send.at[q, d], recv_sem=x_recv.at[q],
            device_id={"blk": lax.rem(x + d, nb)}, device_id_type=MESH)

    def x_wait(q):
        pltpu.make_async_remote_copy(
            src_ref=oldq.at[q], dst_ref=oldq.at[q], send_sem=x_send.at[q, 0], recv_sem=x_recv.at[q],
            device_id={"blk": lax.rem(x + 1, nb)}, device_id_type=MESH).wait_recv()

    for q in order:
        @pl.when(x == q // per)
        def _():
            for d in range(1, nb):
                x_copy(q, d).start()

    label = labels[...]
    y = trait[...]
    y_wide = y.astype(F32)
    masked = jnp.concatenate([jnp.where(label == k, y_wide, 0.0).astype(BF16) for k in range(FOLDS)], axis=0)

    def c_copy(p, right):
        piece = pl.ds(p * cp, cp)
        return pltpu.make_async_remote_copy(
            src_ref=c_send.at[0 if right else 1, piece, :],
            dst_ref=(c_left if right else c_right).at[piece, :],
            send_sem=cs_send.at[0 if right else 1, p], recv_sem=cs_recv.at[0 if right else 1, p],
            device_id={"smp": jnp.minimum(z + 1, n - 1) if right else jnp.maximum(z - 1, 0)}, device_id_type=MESH)

    for b in range(blocks):
        r = jnp.dot(allele[:, b * width:(b + 1) * width], frames[b], preferred_element_type=F32).astype(BF16)
        rot[b] = r
        part[b * c_rows:(b + 1) * c_rows, :] = jnp.dot(masked, r, preferred_element_type=F32)
        for p in range(b * c_rows // cp, (b + 1) * c_rows // cp):
            value = part[p * cp:(p + 1) * cp, :].astype(BF16)

            @pl.when(z == 0)
            def _():
                c_send[0, p * cp:(p + 1) * cp, :] = value
                c_copy(p, True).start()

            @pl.when(z == n - 1)
            def _():
                c_send[1, p * cp:(p + 1) * cp, :] = value
                c_copy(p, False).start()

    for h in range(per):
        oldq[x * per + h] = old[:, h * qw:(h + 1) * qw]
    old_t[...] = old[...].T
    def wait_for(some, who):
        for q in some:
            @pl.when(jnp.logical_and(x != q // per, who))
            def _():
                x_wait(q)

    def g_copy(q, h, right):
        piece = pl.ds(pl.multiple_of(h * gp, gp), gp)
        return pltpu.make_async_remote_copy(
            src_ref=g_send.at[q, piece, :],
            dst_ref=(g_left if right else g_right).at[q, piece, :],
            send_sem=gs_send.at[q, h], recv_sem=(gl_recv if right else gr_recv).at[q, h],
            device_id={"smp": jnp.minimum(z + 1, n - 1) if right else jnp.maximum(z - 1, 0)}, device_id_type=MESH)

    def gram_copy(h):
        piece = pl.ds(pl.multiple_of(h * gp, gp), gp)
        return pltpu.make_async_copy(gram.at[piece, :], gram_out.at[piece, :], gram_sem.at[h])

    def g_piece(q, h):
        piece = pl.ds(pl.multiple_of(h * gp, gp), gp)
        g_part[...] = jnp.dot(old_t[piece, :], oldq[q], preferred_element_type=F32)

        @pl.when(z < q)
        def _():
            @pl.when(z > 0)
            def _():
                g_copy(q, h, True).wait_recv()
                g_part[...] += g_left[q, piece, :].astype(F32)
            g_send[q, piece, :] = g_part[...].astype(BF16)
            g_copy(q, h, True).start()

        @pl.when(z > q)
        def _():
            @pl.when(z < n - 1)
            def _():
                g_copy(q, h, False).wait_recv()
                g_part[...] += g_right[q, piece, :].astype(F32)
            g_send[q, piece, :] = g_part[...].astype(BF16)
            g_copy(q, h, False).start()

        @pl.when(z == q)
        def _():
            @pl.when(z > 0)
            def _():
                g_copy(q, h, True).wait_recv()
                g_part[...] += g_left[q, piece, :].astype(F32)

            @pl.when(z < n - 1)
            def _():
                g_copy(q, h, False).wait_recv()
                g_part[...] += g_right[q, piece, :].astype(F32)
            gram[piece, :] = g_part[...] / sample_total
            gram_copy(h).start()

    def g_group(q):
        def body(h, carry):
            g_piece(q, h)
            return carry
        lax.fori_loop(0, g_pieces, body, 0)

    in_left = z < n // 2
    is_end = jnp.logical_or(z == 0, z == n - 1)

    is_inner = jnp.logical_not(is_end)
    wait_for(order[:2], is_end)
    for i in range(n // 2):
        if i == 1:
            wait_for(order[2:], is_end)

        @pl.when(is_end)
        def _():
            g_group(jnp.where(in_left, n - 1 - i, i))

    def from_side(p, right):
        piece = slice(p * cp, (p + 1) * cp)
        has = z > 0 if right else z < n - 1
        forward = z < n - 1 if right else z > 0

        @pl.when(has)
        def _():
            c_copy(p, right).wait_recv()

            @pl.when(forward)
            def _():
                got = (c_left if right else c_right)[piece, :]
                c_send[0 if right else 1, piece, :] = (part[piece, :] + got.astype(F32)).astype(BF16)
                c_copy(p, right).start()

    for first in (True, False):
        for p in range(c_pieces):
            @pl.when(in_left)
            def _():
                from_side(p, first)

            @pl.when(jnp.logical_not(in_left))
            def _():
                from_side(p, not first)

    wait_for(order, is_inner)

    @pl.when(is_inner)
    def _():
        g_group(jnp.where(in_left, n - 1, 0))

    @pl.when(z > 0)
    def _():
        part[...] += c_left[...].astype(F32)

    @pl.when(z < n - 1)
    def _():
        part[...] += c_right[...].astype(F32)

    sel_rows = lax.broadcasted_iota(jnp.int32, (erows, lams * prot), 0)
    sel_cols = lax.broadcasted_iota(jnp.int32, (erows, lams * prot), 1)
    e0 = jnp.zeros((erows, rows), F32)
    for b in range(blocks):
        damp = [1.0 / (variances[b:b + 1, :] + lam[0:1, r:r + 1]) for r in range(lams)]
        folds = [part[b * c_rows + k * prot:b * c_rows + (k + 1) * prot, :] for k in range(FOLDS)]
        total = folds[0]
        for k in range(1, FOLDS):
            total = total + folds[k]
        acc = jnp.zeros((lams * prot, rows), F32)
        for k in range(FOLDS):
            rest = total - folds[k]
            coeff = jnp.concatenate([(rest * damp[r]).astype(BF16) for r in range(lams)], axis=0)
            acc = jnp.where(
                label == k,
                lax.dot_general(coeff, rot[b], (((1,), (1,)), ((), ())), preferred_element_type=F32),
                acc)
        pred = acc.astype(BF16)
        preds[b * lams * prot:(b + 1) * lams * prot, :] = pred
        wanted = x * new_width + b * lams + sel_cols // prot
        sel = jnp.where(jnp.logical_and(sel_rows == wanted, sel_cols % prot == 0), 1.0, 0.0).astype(BF16)
        e0 = e0 + jnp.dot(sel, pred, preferred_element_type=F32)
    preds_copy = pltpu.make_async_copy(preds, preds_out, out_sem)
    preds_copy.start()
    et_all[x] = e0.astype(BF16)

    def e_copy(d):
        return pltpu.make_async_remote_copy(
            src_ref=et_all.at[x], dst_ref=et_all.at[x], send_sem=e_send.at[d], recv_sem=e_recv.at[d],
            device_id={"blk": lax.rem(x + d, nb)}, device_id_type=MESH)

    def e_wait(d):
        slot = lax.rem(x + nb - d, nb)
        pltpu.make_async_remote_copy(
            src_ref=et_all.at[slot], dst_ref=et_all.at[slot], send_sem=e_send.at[d], recv_sem=e_recv.at[d],
            device_id={"blk": slot}, device_id_type=MESH).wait_recv()

    for d in range(1, nb):
        e_copy(d).start()
    t_rows = lax.broadcasted_iota(jnp.int32, (erows, prot), 0)
    t_cols = lax.broadcasted_iota(jnp.int32, (erows, prot), 1)
    t_sel = jnp.where(jnp.logical_and(t_rows == nb * new_width, t_cols == 0), 1.0, 0.0).astype(BF16)
    target = jnp.dot(t_sel, y, preferred_element_type=F32)
    lhs[...] = (e0 + target).astype(BF16)
    for q in range(n):
        m_send[q, :, :qw] = jnp.dot(lhs[...], oldq[q], preferred_element_type=F32)
    for d in range(1, nb):
        e_wait(d)
    right_side = target
    for b in range(nb):
        right_side = right_side + et_all[b].astype(F32)
    small = lax.dot_general(
        lhs[...], jnp.concatenate([right_side.astype(BF16), jnp.zeros((128 - erows, rows), BF16)], axis=0),
        (((1,), (1,)), ((), ())), preferred_element_type=F32)
    for q in range(n):
        m_send[q, :, qw:] = small

    def m_copy(d):
        return pltpu.make_async_remote_copy(
            src_ref=m_send.at[lax.rem(z + d, n)], dst_ref=m_recv.at[d], send_sem=ms_send.at[d], recv_sem=ms_recv.at[d],
            device_id={"smp": lax.rem(z + d, n)}, device_id_type=MESH)

    for d in range(1, n):
        m_copy(d).start()

    for i in range(n // 2):
        early = jnp.where(in_left, n - 1 - i, i)
        late = n - 1 - early
        if i > 0:
            @pl.when(jnp.logical_and(early != z, is_inner))
            def _():
                g_group(early)

        @pl.when(late != z)
        def _():
            g_group(late)
    g_group(z)

    total = m_send[z]
    for d in range(1, n):
        m_copy(d).wait_recv()
        total = total + m_recv[d]
    small_out[...] = total / sample_total

    preds_copy.wait()
    for h in range(g_pieces):
        gram_copy(h).wait()
    for q in range(n):
        @pl.when(x == q // per)
        def _():
            for d in range(1, nb):
                x_copy(q, d).wait_send()
    for p in range(c_pieces):
        @pl.when(z < n - 1)
        def _():
            c_copy(p, True).wait_send()

        @pl.when(z > 0)
        def _():
            c_copy(p, False).wait_send()
    for d in range(1, nb):
        e_copy(d).wait_send()
    for d in range(1, n):
        m_copy(d).wait_send()
    for q in range(n):
        @pl.when(z != q)
        def _():
            for h in range(g_pieces):
                g_copy(q, h, True).wait_send()


def finish(
    nb, new_width, preds_in, gram_in, small, preds_out, gram_out, cross_out, new_out, fit_old_out, fit_new_out,
    sem
):
    copies = [
        pltpu.make_async_copy(gram_in, gram_out.at[0], sem.at[0]),
        pltpu.make_async_copy(preds_in, preds_out, sem.at[1]),
    ]
    for copy in copies:
        copy.start()
    qw = gram_in.shape[1]
    x = lax.axis_index("blk")
    mine = pl.ds(pl.multiple_of(x * new_width, 8), new_width)
    cross_out[0] = small[mine, :qw]
    new_out[0] = small[mine, qw:qw + nb * new_width]
    fit_old_out[...] = small[nb * new_width:nb * new_width + 1, :qw]
    row = small[nb * new_width:nb * new_width + 1, qw:]
    fit = row[:, :new_width]
    for b in range(1, nb):
        fit = jnp.where(x == b, row[:, b * new_width:(b + 1) * new_width], fit)
    fit_new_out[...] = fit
    for copy in copies:
        copy.wait()


def fused(
    n, nb, allele_matrix, orthonormal_frames, segment_variances, lambda_grid, trait_levels, partition_labels, preceding_fits
):
    rows = allele_matrix.shape[0]
    blocks, width = orthonormal_frames.shape[:2]
    prot = trait_levels.shape[1]
    lams = lambda_grid.shape[0]
    old = preceding_fits[0]
    old_width = old.shape[1]
    qw = old_width * nb // n
    new_width = blocks * lams
    erows = -(-(nb * new_width + 1) // 16) * 16
    c_rows, c_cols = blocks * FOLDS * prot, width
    c_pieces = c_rows // 128
    gp = row_piece(old_width)
    g_pieces = old_width // gp
    vmem = pl.BlockSpec(memory_space=pltpu.VMEM)
    anywhere = pl.BlockSpec(memory_space=pl.ANY)
    dma = pltpu.SemaphoreType.DMA
    out = pl.pallas_call(
        functools.partial(kernel, n, nb, lams),
        out_shape=(
            jax.ShapeDtypeStruct((blocks * lams * prot, rows), BF16),
            jax.ShapeDtypeStruct((old_width, qw), F32),
            jax.ShapeDtypeStruct((erows, qw + 128), F32),
        ),
        in_specs=[vmem] * 7,
        out_specs=(anywhere, anywhere, vmem),
        scratch_shapes=[
            pltpu.VMEM((blocks * lams * prot, rows), BF16),
            pltpu.VMEM((old_width, qw), F32),
            dma, dma((g_pieces,)),
            pltpu.VMEM((n, rows, qw), BF16),
            pltpu.VMEM((old_width, rows), BF16),
            pltpu.VMEM((blocks, rows, width), BF16),
            pltpu.VMEM((c_rows, c_cols), F32),
            pltpu.VMEM((c_rows, c_cols), BF16),
            pltpu.VMEM((c_rows, c_cols), BF16),
            pltpu.VMEM((2, c_rows, c_cols), BF16),
            pltpu.VMEM((n, old_width, qw), BF16),
            pltpu.VMEM((n, old_width, qw), BF16),
            pltpu.VMEM((n, old_width, qw), BF16),
            pltpu.VMEM((gp, qw), F32),
            pltpu.VMEM((nb, erows, rows), BF16),
            pltpu.VMEM((erows, rows), BF16),
            pltpu.VMEM((n, erows, qw + 128), F32),
            pltpu.VMEM((n, erows, qw + 128), F32),
            dma((n, nb)), dma((n,)),
            dma((2, c_pieces)), dma((2, c_pieces)),
            dma((n, g_pieces)), dma((n, g_pieces)), dma((n, g_pieces)),
            dma((nb,)), dma((nb,)), dma((n,)), dma((n,)),
        ],
        compiler_params=pltpu.CompilerParams(
            collective_id=0, has_side_effects=True, vmem_limit_bytes=28 * 1024 * 1024),
        name="ridge",
    )(allele_matrix, orthonormal_frames, segment_variances, lambda_grid[None], trait_levels.T, partition_labels[None], old)
    preds, gram_old, gram_cross, gram_new, fit_old, fit_new = pl.pallas_call(
        functools.partial(finish, nb, new_width),
        out_shape=(
            jax.ShapeDtypeStruct(out[0].shape, BF16),
            jax.ShapeDtypeStruct((1, old_width, qw), F32),
            jax.ShapeDtypeStruct((1, new_width, qw), F32),
            jax.ShapeDtypeStruct((1, new_width, nb * new_width), F32),
            jax.ShapeDtypeStruct((1, qw), F32),
            jax.ShapeDtypeStruct((1, new_width), F32),
        ),
        in_specs=[anywhere, anywhere, vmem],
        out_specs=(anywhere, anywhere, vmem, vmem, vmem, vmem),
        scratch_shapes=[dma((2,))],
        compiler_params=pltpu.CompilerParams(vmem_limit_bytes=4 * 1024 * 1024),
        name="finish",
    )(*out)
    preds = preds.reshape(blocks, lams, prot, rows).transpose(3, 0, 1, 2)
    return preds, gram_old, gram_cross, gram_new, fit_old, fit_new


def segment_fitted_trait(
    projected_traits, pairwise_inner, spectral_line, lambda_grid, partition_mask_real
):
    var_width = projected_traits.shape[1]
    prot_width = pairwise_inner.shape[1] // FOLDS
    lambda_grid_size = lambda_grid.shape[0]
    pairwise_inner = pairwise_inner.reshape(var_width, FOLDS, prot_width)
    remainder = jnp.sum(pairwise_inner, axis=1, keepdims=True) - pairwise_inner
    damping_ratio = 1.0 / (spectral_line[:, None] + lambda_grid[None, :])
    ridge_coefficients = (remainder[:, :, None, :] * damping_ratio[:, None, :, None]).astype(
        jnp.bfloat16
    )
    row_count = projected_traits.shape[0]
    running_total = jnp.zeros((row_count, lambda_grid_size * prot_width), jnp.float32)
    for holdout_index in range(FOLDS):
        lookup_table = ridge_coefficients[:, holdout_index].reshape(
            var_width, lambda_grid_size * prot_width
        )
        running_total = running_total + partition_mask_real[
            :, holdout_index : holdout_index + 1
        ] * jnp.dot(projected_traits, lookup_table, preferred_element_type=jnp.float32)
    return running_total.reshape(row_count, lambda_grid_size, prot_width).astype(jnp.bfloat16)


def sum_block(local_cross):
    return lax.psum(local_cross, "smp")


def per_device(
    allele_matrix,
    orthonormal_frames,
    segment_variances,
    lambda_grid,
    trait_levels,
    partition_labels,
    preceding_fits,
):
    row_count = allele_matrix.shape[0]
    block_count = orthonormal_frames.shape[0]
    var_width = orthonormal_frames.shape[1]
    prot_width = trait_levels.shape[1]
    lambda_grid_size = lambda_grid.shape[0]
    sample_total = float(row_count * lax.axis_size("smp"))
    contract = (((0,), (0,)), ((), ()))
    member = partition_labels[:, None] == jnp.arange(FOLDS, dtype=jnp.int32)[None, :]
    partition_mask_real = member.astype(jnp.float32)
    masked = (member.astype(jnp.bfloat16)[:, :, None] * trait_levels[:, None, :]).reshape(
        row_count, FOLDS * prot_width
    )
    rotated_list = []
    local_list = []
    for entry_offset in range(block_count):
        genotype_cols = allele_matrix[:, entry_offset * var_width : (entry_offset + 1) * var_width]
        projected_traits = jnp.dot(
            genotype_cols, orthonormal_frames[entry_offset], preferred_element_type=jnp.float32
        ).astype(jnp.bfloat16)
        rotated_list.append(projected_traits)
        local_list.append(
            lax.dot_general(projected_traits, masked, contract, preferred_element_type=jnp.float32)
        )
    crossed_list = [sum_block(local_cross) for local_cross in local_list]
    pred_list = [
        segment_fitted_trait(
            rotated_list[entry_offset],
            crossed_list[entry_offset],
            segment_variances[entry_offset],
            lambda_grid,
            partition_mask_real,
        )
        for entry_offset in range(block_count)
    ]
    level0_predictions = jnp.stack(pred_list, axis=1)
    added_columns = level0_predictions[:, :, :, 0].reshape(
        row_count, block_count * lambda_grid_size
    )
    target = trait_levels[:, 0:1]
    old_cols = preceding_fits[0]
    old_width = old_cols.shape[1]
    new_width = added_columns.shape[1]
    joined = jnp.concatenate([old_cols, added_columns], axis=1)
    gathered = lax.all_gather(joined, "blk", axis=1, tiled=True)
    shard_count = gathered.shape[1] // joined.shape[1]
    pieces = gathered.reshape(row_count, shard_count, joined.shape[1])
    old_all = pieces[:, :, :old_width].reshape(row_count, shard_count * old_width)
    new_all = pieces[:, :, old_width:].reshape(row_count, shard_count * new_width)
    stacked = jnp.concatenate([old_cols, added_columns, target], axis=1)
    reduced = lax.psum_scatter(
        lax.dot_general(stacked, old_all, contract, preferred_element_type=jnp.float32),
        "smp",
        scatter_dimension=1,
        tiled=True,
    )
    gram_old = reduced[:old_width]
    gram_cross = reduced[old_width : old_width + new_width]
    fit_old = reduced[old_width + new_width :]
    right_side = jnp.concatenate([new_all, target], axis=1)
    small_gram = lax.psum(
        lax.dot_general(added_columns, right_side, contract, preferred_element_type=jnp.float32),
        "smp",
    )
    gram_new = small_gram[:, :-1]
    fit_new = small_gram[:, -1]
    return (
        level0_predictions,
        (gram_old / sample_total)[None],
        (gram_cross / sample_total)[None],
        (gram_new / sample_total)[None],
        fit_old / sample_total,
        (fit_new / sample_total)[None],
    )


def solution(mesh):
    n, nb = mesh.shape["smp"], mesh.shape["blk"]

    def program(*arrays):
        _, frames, _, lambda_grid, trait_levels, _, preceding_fits = arrays
        old_width = preceding_fits.shape[2]
        new_width = frames.shape[0] * lambda_grid.shape[0]
        fits = (
            n % 2 == 0
            and n % nb == 0
            and (old_width * nb) % (n * 128) == 0
            and frames.shape[1] % 128 == 0
            and new_width % 8 == 0
            and old_width % 64 == 0
            and FOLDS * trait_levels.shape[1] % 128 == 0
            and nb * new_width < 128
        )
        if fits:
            return fused(n, nb, *arrays)
        return per_device(*arrays)

    placed = (
        P("smp", ("grp", "blk")),
        P(("grp", "blk"), None, None),
        P(("grp", "blk"), None),
        P(),
        P("smp", ("grp", "pen")),
        P("smp"),
        P(("grp", "pen"), "smp", "blk"),
    )
    return jax.shard_map(
        program,
        mesh=mesh,
        in_specs=placed,
        out_specs=(
            P("smp", ("grp", "blk"), None, "pen"),
            P(("grp", "pen"), "blk", "smp"),
            P(("grp", "pen"), "blk", "smp"),
            P(("grp", "pen"), "blk", None),
            P(("grp", "pen"), "smp"),
            P(("grp", "pen"), "blk"),
        ),
        check_vma=False,
    )
```

```python
import functools

import jax
import jax.numpy as jnp
from jax import lax
from jax.experimental import pallas as pl
from jax.experimental.pallas import tpu as pltpu
from jax.sharding import PartitionSpec as P

FOLDS = 4
F32 = jnp.float32
BF16 = jnp.bfloat16
MESH = pl.DeviceIdType.MESH


def row_piece(total):
    return next(size for size in (256, 128) if total % size == 0)


def kernel(
    n, nb, groups,
    allele_in, frames_in, variances_in, lam_in, trait_in, labels_in, old_in,
    preds_out, gram_out, small_out,
    allele, frames, variances, lam, trait, labels, old, preds, gram, in_sem, out_sem, gram_sem,
    oldq, old_t, rot, part, c_left, c_right, c_send,
    g_left, g_right, g_send, g_part, et_all, lhs, m_send, m_recv,
    x_send, x_recv, cs_send, cs_recv, gs_send, gl_recv, gr_recv,
    e_send, e_recv, ms_send, ms_recv,
):
    z = lax.axis_index("smp")
    x = lax.axis_index("blk")
    rows, old_width = old.shape
    blocks, width = frames.shape[0], frames.shape[1]
    prot = trait.shape[0]
    lams = groups
    per = n // nb
    qw = old_width // per
    c_rows = FOLDS * prot
    cp = 128
    c_pieces = blocks * c_rows // cp
    gp = row_piece(old_width)
    g_pieces = old_width // gp
    new_width = blocks * lams
    erows = et_all.shape[1]
    sample_total = float(rows * n)
    order = []
    for i in range(n // 2):
        order += [n - 1 - i, i]

    loads = [
        pltpu.make_async_copy(source, place, in_sem.at[i])
        for i, (source, place) in enumerate((
            (allele_in, allele), (frames_in, frames), (trait_in, trait), (labels_in, labels),
            (old_in, old), (variances_in, variances), (lam_in, lam)))
    ]
    for load in loads:
        load.start()
    barrier = pltpu.get_barrier_semaphore()
    for d in range(1, n):
        pl.semaphore_signal(barrier, inc=1, device_id={"smp": lax.rem(z + d, n)}, device_id_type=MESH)
    for d in range(1, nb):
        pl.semaphore_signal(barrier, inc=1, device_id={"blk": lax.rem(x + d, nb)}, device_id_type=MESH)
    pl.semaphore_wait(barrier, n - 1 + nb - 1)

    def x_copy(q, d):
        cols = pl.ds(pl.multiple_of((q - x * per) * qw, qw), qw)
        return pltpu.make_async_remote_copy(
            src_ref=old_in.at[:, cols], dst_ref=oldq.at[q], send_sem=x_send.at[q, d], recv_sem=x_recv.at[q],
            device_id={"blk": lax.rem(x + d, nb)}, device_id_type=MESH)

    def x_wait(q):
        pltpu.make_async_remote_copy(
            src_ref=oldq.at[q], dst_ref=oldq.at[q], send_sem=x_send.at[q, 0], recv_sem=x_recv.at[q],
            device_id={"blk": lax.rem(x + 1, nb)}, device_id_type=MESH).wait_recv()

    for q in order:
        @pl.when(x == q // per)
        def _():
            for d in range(1, nb):
                x_copy(q, d).start()

    for load in loads[:4]:
        load.wait()
    label = labels[...]
    y = trait[...]
    y_wide = y.astype(F32)
    masked = jnp.concatenate([jnp.where(label == k, y_wide, 0.0).astype(BF16) for k in range(FOLDS)], axis=0)

    def c_copy(p, right):
        piece = pl.ds(p * cp, cp)
        return pltpu.make_async_remote_copy(
            src_ref=c_send.at[0 if right else 1, piece, :],
            dst_ref=(c_left if right else c_right).at[piece, :],
            send_sem=cs_send.at[0 if right else 1, p], recv_sem=cs_recv.at[0 if right else 1, p],
            device_id={"smp": jnp.minimum(z + 1, n - 1) if right else jnp.maximum(z - 1, 0)}, device_id_type=MESH)

    for b in range(blocks):
        r = jnp.dot(allele[:, b * width:(b + 1) * width], frames[b], preferred_element_type=F32).astype(BF16)
        rot[b] = r
        part[b * c_rows:(b + 1) * c_rows, :] = jnp.dot(masked, r, preferred_element_type=F32)
        for p in range(b * c_rows // cp, (b + 1) * c_rows // cp):
            value = part[p * cp:(p + 1) * cp, :].astype(BF16)

            @pl.when(z == 0)
            def _():
                c_send[0, p * cp:(p + 1) * cp, :] = value
                c_copy(p, True).start()

            @pl.when(z == n - 1)
            def _():
                c_send[1, p * cp:(p + 1) * cp, :] = value
                c_copy(p, False).start()

    for load in loads[4:]:
        load.wait()
    for h in range(per):
        oldq[x * per + h] = old[:, h * qw:(h + 1) * qw]
    old_t[...] = old[...].T
    def wait_for(some, who):
        for q in some:
            @pl.when(jnp.logical_and(x != q // per, who))
            def _():
                x_wait(q)

    def g_copy(q, h, right):
        piece = pl.ds(pl.multiple_of(h * gp, gp), gp)
        return pltpu.make_async_remote_copy(
            src_ref=g_send.at[q, piece, :],
            dst_ref=(g_left if right else g_right).at[q, piece, :],
            send_sem=gs_send.at[q, h], recv_sem=(gl_recv if right else gr_recv).at[q, h],
            device_id={"smp": jnp.minimum(z + 1, n - 1) if right else jnp.maximum(z - 1, 0)}, device_id_type=MESH)

    def gram_copy(h):
        piece = pl.ds(pl.multiple_of(h * gp, gp), gp)
        return pltpu.make_async_copy(gram.at[piece, :], gram_out.at[piece, :], gram_sem.at[h])

    def g_piece(q, h):
        piece = pl.ds(pl.multiple_of(h * gp, gp), gp)
        g_part[...] = jnp.dot(old_t[piece, :], oldq[q], preferred_element_type=F32)

        @pl.when(z < q)
        def _():
            @pl.when(z > 0)
            def _():
                g_copy(q, h, True).wait_recv()
                g_part[...] += g_left[q, piece, :].astype(F32)
            g_send[q, piece, :] = g_part[...].astype(BF16)
            g_copy(q, h, True).start()

        @pl.when(z > q)
        def _():
            @pl.when(z < n - 1)
            def _():
                g_copy(q, h, False).wait_recv()
                g_part[...] += g_right[q, piece, :].astype(F32)
            g_send[q, piece, :] = g_part[...].astype(BF16)
            g_copy(q, h, False).start()

        @pl.when(z == q)
        def _():
            @pl.when(z > 0)
            def _():
                g_copy(q, h, True).wait_recv()
                g_part[...] += g_left[q, piece, :].astype(F32)

            @pl.when(z < n - 1)
            def _():
                g_copy(q, h, False).wait_recv()
                g_part[...] += g_right[q, piece, :].astype(F32)
            gram[piece, :] = g_part[...] / sample_total
            gram_copy(h).start()

    def g_group(q):
        def body(h, carry):
            g_piece(q, h)
            return carry
        lax.fori_loop(0, g_pieces, body, 0)

    in_left = z < n // 2
    is_end = jnp.logical_or(z == 0, z == n - 1)

    is_inner = jnp.logical_not(is_end)
    wait_for(order[:2], is_end)
    for i in range(n // 2):
        if i == 1:
            wait_for(order[2:], is_end)

        @pl.when(is_end)
        def _():
            g_group(jnp.where(in_left, n - 1 - i, i))

    def from_side(p, right):
        piece = slice(p * cp, (p + 1) * cp)
        has = z > 0 if right else z < n - 1
        forward = z < n - 1 if right else z > 0

        @pl.when(has)
        def _():
            c_copy(p, right).wait_recv()

            @pl.when(forward)
            def _():
                got = (c_left if right else c_right)[piece, :]
                c_send[0 if right else 1, piece, :] = (part[piece, :] + got.astype(F32)).astype(BF16)
                c_copy(p, right).start()

    for first in (True, False):
        for p in range(c_pieces):
            @pl.when(in_left)
            def _():
                from_side(p, first)

            @pl.when(jnp.logical_not(in_left))
            def _():
                from_side(p, not first)

    wait_for(order, is_inner)

    @pl.when(is_inner)
    def _():
        g_group(jnp.where(in_left, n - 1, 0))

    @pl.when(z > 0)
    def _():
        part[...] += c_left[...].astype(F32)

    @pl.when(z < n - 1)
    def _():
        part[...] += c_right[...].astype(F32)

    sel_rows = lax.broadcasted_iota(jnp.int32, (erows, lams * prot), 0)
    sel_cols = lax.broadcasted_iota(jnp.int32, (erows, lams * prot), 1)
    e0 = jnp.zeros((erows, rows), F32)
    for b in range(blocks):
        damp = [1.0 / (variances[b:b + 1, :] + lam[0:1, r:r + 1]) for r in range(lams)]
        folds = [part[b * c_rows + k * prot:b * c_rows + (k + 1) * prot, :] for k in range(FOLDS)]
        total = folds[0]
        for k in range(1, FOLDS):
            total = total + folds[k]
        acc = jnp.zeros((lams * prot, rows), F32)
        for k in range(FOLDS):
            rest = total - folds[k]
            coeff = jnp.concatenate([(rest * damp[r]).astype(BF16) for r in range(lams)], axis=0)
            acc = jnp.where(
                label == k,
                lax.dot_general(coeff, rot[b], (((1,), (1,)), ((), ())), preferred_element_type=F32),
                acc)
        pred = acc.astype(BF16)
        preds[b * lams * prot:(b + 1) * lams * prot, :] = pred
        wanted = x * new_width + b * lams + sel_cols // prot
        sel = jnp.where(jnp.logical_and(sel_rows == wanted, sel_cols % prot == 0), 1.0, 0.0).astype(BF16)
        e0 = e0 + jnp.dot(sel, pred, preferred_element_type=F32)
    preds_copy = pltpu.make_async_copy(preds, preds_out, out_sem)
    preds_copy.start()
    et_all[x] = e0.astype(BF16)

    def e_copy(d):
        return pltpu.make_async_remote_copy(
            src_ref=et_all.at[x], dst_ref=et_all.at[x], send_sem=e_send.at[d], recv_sem=e_recv.at[d],
            device_id={"blk": lax.rem(x + d, nb)}, device_id_type=MESH)

    def e_wait(d):
        slot = lax.rem(x + nb - d, nb)
        pltpu.make_async_remote_copy(
            src_ref=et_all.at[slot], dst_ref=et_all.at[slot], send_sem=e_send.at[d], recv_sem=e_recv.at[d],
            device_id={"blk": slot}, device_id_type=MESH).wait_recv()

    for d in range(1, nb):
        e_copy(d).start()
    t_rows = lax.broadcasted_iota(jnp.int32, (erows, prot), 0)
    t_cols = lax.broadcasted_iota(jnp.int32, (erows, prot), 1)
    t_sel = jnp.where(jnp.logical_and(t_rows == nb * new_width, t_cols == 0), 1.0, 0.0).astype(BF16)
    target = jnp.dot(t_sel, y, preferred_element_type=F32)
    lhs[...] = (e0 + target).astype(BF16)
    for q in range(n):
        m_send[q, :, :qw] = jnp.dot(lhs[...], oldq[q], preferred_element_type=F32)
    for d in range(1, nb):
        e_wait(d)
    right_side = target
    for b in range(nb):
        right_side = right_side + et_all[b].astype(F32)
    small = lax.dot_general(
        lhs[...], jnp.concatenate([right_side.astype(BF16), jnp.zeros((128 - erows, rows), BF16)], axis=0),
        (((1,), (1,)), ((), ())), preferred_element_type=F32)
    for q in range(n):
        m_send[q, :, qw:] = small

    def m_copy(d):
        return pltpu.make_async_remote_copy(
            src_ref=m_send.at[lax.rem(z + d, n)], dst_ref=m_recv.at[d], send_sem=ms_send.at[d], recv_sem=ms_recv.at[d],
            device_id={"smp": lax.rem(z + d, n)}, device_id_type=MESH)

    for d in range(1, n):
        m_copy(d).start()

    for i in range(n // 2):
        early = jnp.where(in_left, n - 1 - i, i)
        late = n - 1 - early
        if i > 0:
            @pl.when(jnp.logical_and(early != z, is_inner))
            def _():
                g_group(early)

        @pl.when(late != z)
        def _():
            g_group(late)
    g_group(z)

    total = m_send[z]
    for d in range(1, n):
        m_copy(d).wait_recv()
        total = total + m_recv[d]
    small_out[...] = total / sample_total

    preds_copy.wait()
    for h in range(g_pieces):
        gram_copy(h).wait()
    for q in range(n):
        @pl.when(x == q // per)
        def _():
            for d in range(1, nb):
                x_copy(q, d).wait_send()
    for p in range(c_pieces):
        @pl.when(z < n - 1)
        def _():
            c_copy(p, True).wait_send()

        @pl.when(z > 0)
        def _():
            c_copy(p, False).wait_send()
    for d in range(1, nb):
        e_copy(d).wait_send()
    for d in range(1, n):
        m_copy(d).wait_send()
    for q in range(n):
        @pl.when(z != q)
        def _():
            for h in range(g_pieces):
                g_copy(q, h, True).wait_send()


def finish(
    nb, new_width, preds_in, gram_in, small, preds_out, gram_out, cross_out, new_out, fit_old_out, fit_new_out,
    sem
):
    copies = [
        pltpu.make_async_copy(gram_in, gram_out.at[0], sem.at[0]),
        pltpu.make_async_copy(preds_in, preds_out, sem.at[1]),
    ]
    for copy in copies:
        copy.start()
    qw = gram_in.shape[1]
    x = lax.axis_index("blk")
    mine = pl.ds(pl.multiple_of(x * new_width, 8), new_width)
    cross_out[0] = small[mine, :qw]
    new_out[0] = small[mine, qw:qw + nb * new_width]
    fit_old_out[...] = small[nb * new_width:nb * new_width + 1, :qw]
    row = small[nb * new_width:nb * new_width + 1, qw:]
    fit = row[:, :new_width]
    for b in range(1, nb):
        fit = jnp.where(x == b, row[:, b * new_width:(b + 1) * new_width], fit)
    fit_new_out[...] = fit
    for copy in copies:
        copy.wait()


def fused(
    n, nb, allele_matrix, orthonormal_frames, segment_variances, lambda_grid, trait_levels, partition_labels, preceding_fits
):
    rows = allele_matrix.shape[0]
    blocks, width = orthonormal_frames.shape[:2]
    prot = trait_levels.shape[1]
    lams = lambda_grid.shape[0]
    old = preceding_fits[0]
    old_width = old.shape[1]
    qw = old_width * nb // n
    new_width = blocks * lams
    erows = -(-(nb * new_width + 1) // 16) * 16
    c_rows, c_cols = blocks * FOLDS * prot, width
    c_pieces = c_rows // 128
    gp = row_piece(old_width)
    g_pieces = old_width // gp
    vmem = pl.BlockSpec(memory_space=pltpu.VMEM)
    anywhere = pl.BlockSpec(memory_space=pl.ANY)
    dma = pltpu.SemaphoreType.DMA
    out = pl.pallas_call(
        functools.partial(kernel, n, nb, lams),
        out_shape=(
            jax.ShapeDtypeStruct((blocks * lams * prot, rows), BF16),
            jax.ShapeDtypeStruct((old_width, qw), F32),
            jax.ShapeDtypeStruct((erows, qw + 128), F32),
        ),
        in_specs=[pl.BlockSpec(memory_space=pltpu.HBM)] * 7,
        out_specs=(anywhere, anywhere, vmem),
        scratch_shapes=[
            pltpu.VMEM(allele_matrix.shape, BF16),
            pltpu.VMEM(orthonormal_frames.shape, BF16),
            pltpu.VMEM(segment_variances.shape, F32),
            pltpu.VMEM((1, lams), F32),
            pltpu.VMEM((prot, rows), BF16),
            pltpu.VMEM((1, rows), jnp.int32),
            pltpu.VMEM(old.shape, BF16),
            pltpu.VMEM((blocks * lams * prot, rows), BF16),
            pltpu.VMEM((old_width, qw), F32),
            dma((7,)), dma, dma((g_pieces,)),
            pltpu.VMEM((n, rows, qw), BF16),
            pltpu.VMEM((old_width, rows), BF16),
            pltpu.VMEM((blocks, rows, width), BF16),
            pltpu.VMEM((c_rows, c_cols), F32),
            pltpu.VMEM((c_rows, c_cols), BF16),
            pltpu.VMEM((c_rows, c_cols), BF16),
            pltpu.VMEM((2, c_rows, c_cols), BF16),
            pltpu.VMEM((n, old_width, qw), BF16),
            pltpu.VMEM((n, old_width, qw), BF16),
            pltpu.VMEM((n, old_width, qw), BF16),
            pltpu.VMEM((gp, qw), F32),
            pltpu.VMEM((nb, erows, rows), BF16),
            pltpu.VMEM((erows, rows), BF16),
            pltpu.VMEM((n, erows, qw + 128), F32),
            pltpu.VMEM((n, erows, qw + 128), F32),
            dma((n, nb)), dma((n,)),
            dma((2, c_pieces)), dma((2, c_pieces)),
            dma((n, g_pieces)), dma((n, g_pieces)), dma((n, g_pieces)),
            dma((nb,)), dma((nb,)), dma((n,)), dma((n,)),
        ],
        compiler_params=pltpu.CompilerParams(
            collective_id=0, has_side_effects=True, vmem_limit_bytes=28 * 1024 * 1024),
        name="ridge",
    )(*[
        pltpu.with_memory_space_constraint(array, pltpu.HBM)
        for array in (
            allele_matrix, orthonormal_frames, segment_variances, lambda_grid[None], trait_levels.T,
            partition_labels[None], old)
    ])
    preds, gram_old, gram_cross, gram_new, fit_old, fit_new = pl.pallas_call(
        functools.partial(finish, nb, new_width),
        out_shape=(
            jax.ShapeDtypeStruct(out[0].shape, BF16),
            jax.ShapeDtypeStruct((1, old_width, qw), F32),
            jax.ShapeDtypeStruct((1, new_width, qw), F32),
            jax.ShapeDtypeStruct((1, new_width, nb * new_width), F32),
            jax.ShapeDtypeStruct((1, qw), F32),
            jax.ShapeDtypeStruct((1, new_width), F32),
        ),
        in_specs=[anywhere, anywhere, vmem],
        out_specs=(anywhere, anywhere, vmem, vmem, vmem, vmem),
        scratch_shapes=[dma((2,))],
        compiler_params=pltpu.CompilerParams(vmem_limit_bytes=4 * 1024 * 1024),
        name="finish",
    )(*out)
    preds = preds.reshape(blocks, lams, prot, rows).transpose(3, 0, 1, 2)
    return preds, gram_old, gram_cross, gram_new, fit_old, fit_new


def segment_fitted_trait(
    projected_traits, pairwise_inner, spectral_line, lambda_grid, partition_mask_real
):
    var_width = projected_traits.shape[1]
    prot_width = pairwise_inner.shape[1] // FOLDS
    lambda_grid_size = lambda_grid.shape[0]
    pairwise_inner = pairwise_inner.reshape(var_width, FOLDS, prot_width)
    remainder = jnp.sum(pairwise_inner, axis=1, keepdims=True) - pairwise_inner
    damping_ratio = 1.0 / (spectral_line[:, None] + lambda_grid[None, :])
    ridge_coefficients = (remainder[:, :, None, :] * damping_ratio[:, None, :, None]).astype(
        jnp.bfloat16
    )
    row_count = projected_traits.shape[0]
    running_total = jnp.zeros((row_count, lambda_grid_size * prot_width), jnp.float32)
    for holdout_index in range(FOLDS):
        lookup_table = ridge_coefficients[:, holdout_index].reshape(
            var_width, lambda_grid_size * prot_width
        )
        running_total = running_total + partition_mask_real[
            :, holdout_index : holdout_index + 1
        ] * jnp.dot(projected_traits, lookup_table, preferred_element_type=jnp.float32)
    return running_total.reshape(row_count, lambda_grid_size, prot_width).astype(jnp.bfloat16)


def sum_block(local_cross):
    return lax.psum(local_cross, "smp")


def per_device(
    allele_matrix,
    orthonormal_frames,
    segment_variances,
    lambda_grid,
    trait_levels,
    partition_labels,
    preceding_fits,
):
    row_count = allele_matrix.shape[0]
    block_count = orthonormal_frames.shape[0]
    var_width = orthonormal_frames.shape[1]
    prot_width = trait_levels.shape[1]
    lambda_grid_size = lambda_grid.shape[0]
    sample_total = float(row_count * lax.axis_size("smp"))
    contract = (((0,), (0,)), ((), ()))
    member = partition_labels[:, None] == jnp.arange(FOLDS, dtype=jnp.int32)[None, :]
    partition_mask_real = member.astype(jnp.float32)
    masked = (member.astype(jnp.bfloat16)[:, :, None] * trait_levels[:, None, :]).reshape(
        row_count, FOLDS * prot_width
    )
    rotated_list = []
    local_list = []
    for entry_offset in range(block_count):
        genotype_cols = allele_matrix[:, entry_offset * var_width : (entry_offset + 1) * var_width]
        projected_traits = jnp.dot(
            genotype_cols, orthonormal_frames[entry_offset], preferred_element_type=jnp.float32
        ).astype(jnp.bfloat16)
        rotated_list.append(projected_traits)
        local_list.append(
            lax.dot_general(projected_traits, masked, contract, preferred_element_type=jnp.float32)
        )
    crossed_list = [sum_block(local_cross) for local_cross in local_list]
    pred_list = [
        segment_fitted_trait(
            rotated_list[entry_offset],
            crossed_list[entry_offset],
            segment_variances[entry_offset],
            lambda_grid,
            partition_mask_real,
        )
        for entry_offset in range(block_count)
    ]
    level0_predictions = jnp.stack(pred_list, axis=1)
    added_columns = level0_predictions[:, :, :, 0].reshape(
        row_count, block_count * lambda_grid_size
    )
    target = trait_levels[:, 0:1]
    old_cols = preceding_fits[0]
    old_width = old_cols.shape[1]
    new_width = added_columns.shape[1]
    joined = jnp.concatenate([old_cols, added_columns], axis=1)
    gathered = lax.all_gather(joined, "blk", axis=1, tiled=True)
    shard_count = gathered.shape[1] // joined.shape[1]
    pieces = gathered.reshape(row_count, shard_count, joined.shape[1])
    old_all = pieces[:, :, :old_width].reshape(row_count, shard_count * old_width)
    new_all = pieces[:, :, old_width:].reshape(row_count, shard_count * new_width)
    stacked = jnp.concatenate([old_cols, added_columns, target], axis=1)
    reduced = lax.psum_scatter(
        lax.dot_general(stacked, old_all, contract, preferred_element_type=jnp.float32),
        "smp",
        scatter_dimension=1,
        tiled=True,
    )
    gram_old = reduced[:old_width]
    gram_cross = reduced[old_width : old_width + new_width]
    fit_old = reduced[old_width + new_width :]
    right_side = jnp.concatenate([new_all, target], axis=1)
    small_gram = lax.psum(
        lax.dot_general(added_columns, right_side, contract, preferred_element_type=jnp.float32),
        "smp",
    )
    gram_new = small_gram[:, :-1]
    fit_new = small_gram[:, -1]
    return (
        level0_predictions,
        (gram_old / sample_total)[None],
        (gram_cross / sample_total)[None],
        (gram_new / sample_total)[None],
        fit_old / sample_total,
        (fit_new / sample_total)[None],
    )


def solution(mesh):
    n, nb = mesh.shape["smp"], mesh.shape["blk"]

    def program(*arrays):
        _, frames, _, lambda_grid, trait_levels, _, preceding_fits = arrays
        old_width = preceding_fits.shape[2]
        new_width = frames.shape[0] * lambda_grid.shape[0]
        fits = (
            n % 2 == 0
            and n % nb == 0
            and (old_width * nb) % (n * 128) == 0
            and frames.shape[1] % 128 == 0
            and new_width % 8 == 0
            and old_width % 64 == 0
            and FOLDS * trait_levels.shape[1] % 128 == 0
            and nb * new_width < 128
        )
        if fits:
            return fused(n, nb, *arrays)
        return per_device(*arrays)

    placed = (
        P("smp", ("grp", "blk")),
        P(("grp", "blk"), None, None),
        P(("grp", "blk"), None),
        P(),
        P("smp", ("grp", "pen")),
        P("smp"),
        P(("grp", "pen"), "smp", "blk"),
    )
    return jax.shard_map(
        program,
        mesh=mesh,
        in_specs=placed,
        out_specs=(
            P("smp", ("grp", "blk"), None, "pen"),
            P(("grp", "pen"), "blk", "smp"),
            P(("grp", "pen"), "blk", "smp"),
            P(("grp", "pen"), "blk", None),
            P(("grp", "pen"), "smp"),
            P(("grp", "pen"), "blk"),
        ),
        check_vma=False,
    )
```
